32 devices in a mesh: dp: 8 (over y, x, core), expert: 4 (over z).
Axes of the slice: x: 2, y: 2, z: 4, core: 2. Of those that a mesh axis runs over, the one named last changes fastest.
Arguments:
- out_grad: bfloat16 [8, 1024, 2048], P('dp', 'expert'), may hold values from -6 to 6
- gates: bfloat16 [8, 1024, 8], P('dp', 'expert'), may hold values from 0.019897461 to 0.5
- expert_ids: int32 [8, 1024, 8], P('dp', 'expert'), may hold values from 0 to 127, as said below
- route_slots: int32 [8, 1024, 8], P('dp', 'expert'), may hold values from -1 to 20, as said below
- saved_hidden: bfloat16 [8, 4, 84, 768], P('dp', 'expert'), may hold values from -0.21582031 to 0.21582031
- down_weight: bfloat16 [4, 768, 2048], P('expert'), may hold values from -0.21875 to 0.21875
Outputs:
- hidden_grad: bfloat16 [8, 4, 84, 768], P('dp', 'expert')
- weight_grad: float32 [4, 768, 2048], P('expert', 'dp')
- gate_grad: float32 [8, 1024, 8], P('dp', 'expert')
The draws below stay inside these ranges and needn't reach their ends.
Inputs may be any that keep to these rules, and one draw needn't show every extreme that they name: `expert_ids`: each token names 8 different experts. `route_slots`: for each replica, each block of 256 tokens and each expert e below 4, the routes of that block to e that have a slot take the numbers 0, 1, 2 and on without gaps in the order of tokens and ranks, at most 21 of them; routes to experts 4 and above have -1. In every replica some expert below 4 holds 21 routes from every block, and routes beyond that are -1.
All inputs are finite; a program needn't handle non-finite values.
Results may differ from the reference program's by a relative error of at most 0.0095.
Values may be sent and summed in bfloat16 or wider, within the bound.
No kernel may reach another device: no remote copies, remote signals or barrier semaphores. Data moves between devices by JAX's collectives and lax.ppermute only.
A program may use at most 64 MiB of HBM per device.

```python
import jax
import jax.numpy as jnp
from jax import lax

DW = 2048
HW = 768
EXPERTS = 128
TOPK = 8
TOK_DEV = 256
C_SRC = 21
EXP_WIN = 4
SLOTS = 84
TOKENS = 1024
REPLICAS = 8


def routing_tables(key):
    key_scores, key_hot = jax.random.split(jax.random.fold_in(key, 7), 2)
    scores = jax.random.randint(key_scores, (REPLICAS, TOKENS, EXPERTS), 0, 2 ** 20, dtype=jnp.int32)
    scores = scores * EXPERTS + jnp.arange(EXPERTS, dtype=jnp.int32)[None, None, :]
    hot_expert = jax.random.randint(key_hot, (REPLICAS,), 0, EXP_WIN, dtype=jnp.int32)
    position = jnp.arange(TOKENS, dtype=jnp.int32) % TOK_DEV
    favoured = (position[None, :, None] <= C_SRC) & (jnp.arange(EXPERTS, dtype=jnp.int32)[None, None, :] == hot_expert[:, None, None])
    scores = scores + favoured.astype(jnp.int32) * 2 ** 28
    chosen_scores, expert_ids = lax.top_k(scores, TOPK)
    expert_ids = expert_ids.astype(jnp.int32)
    blocks = expert_ids.reshape(REPLICAS, EXP_WIN, TOK_DEV * TOPK)
    onehot = (blocks[..., None] == jnp.arange(EXP_WIN, dtype=jnp.int32)).astype(jnp.int32)
    ranks = jnp.cumsum(onehot, axis=2) - 1
    rank_taken = jnp.sum(onehot * ranks, axis=-1)
    inside = (blocks < EXP_WIN) & (rank_taken < C_SRC)
    route_slots = jnp.where(inside, rank_taken, -1).astype(jnp.int32).reshape(REPLICAS, TOKENS, TOPK)
    return (expert_ids, route_slots)


def draw_expert_ids(key, part):
    return routing_tables(key)[0]


def draw_route_slots(key, part):
    return routing_tables(key)[1]


def raised(values, rng, source, target, parts, factor):
    owner, partner = [(jnp.arange(values.shape[dim]) // (values.shape[dim] // parts)).reshape([-1 if axis == dim else 1 for axis in range(values.ndim)]) for dim in (source, target)]
    chosen = jax.random.permutation(rng, parts)[partner]
    strong = (owner == chosen) | (owner == (partner + parts // 2) % parts)
    return jnp.where(strong, factor * values, values)


def level_of(rng, extent, cuts, low, largest):
    loudness = 1.0
    for dim, shards_of in cuts:
        heights = jax.random.uniform(jax.random.fold_in(jax.random.fold_in(rng, 6), dim), (shards_of,), jnp.float32, low / len(cuts), largest / len(cuts))
        loudness = loudness * jnp.repeat(jnp.exp(heights), extent[dim] // shards_of).reshape((-1,) + (1,) * (len(extent) - 1 - dim))
    return loudness


def noise(key, shape, width, reach, cuts=(), held_as=jnp.bfloat16):
    loudness = level_of(key, shape, cuts, -0.22, 0.18) if cuts else 1.0
    values = jax.random.normal(key, shape, jnp.float32) * width * loudness
    return jnp.minimum(jnp.maximum(values, -reach), reach).astype(held_as)


def heavy_noise(key, extent, spread, bound, pieces, heavy, kind=jnp.bfloat16):
    values = spread * jax.random.normal(key, extent, jnp.float32)
    if pieces:
        values = values * level_of(key, extent, pieces, -0.22, 0.18)
    return jnp.clip(raised(values, jax.random.fold_in(key, 3), *heavy), -bound, bound).astype(kind)


def setup_inputs(seed: int = 0) -> dict:
    seeds = jax.random.split(jax.random.key(seed), 7)
    out_grad = noise(seeds[0], (REPLICAS, TOKENS, DW), 1.0, 6.0, ((0, 8), (1, 4)))
    gates = jnp.clip(0.019897461 + 0.48010254 * jax.random.uniform(seeds[1], (REPLICAS, TOKENS, TOPK), jnp.float32) ** level_of(seeds[1], (REPLICAS, TOKENS, TOPK), ((0, 8), (1, 4)), -0.2, 0.2), 0.019897461, 0.5).astype(jnp.bfloat16)
    expert_ids = draw_expert_ids(jax.random.fold_in(seeds[6], 71), 0)
    route_slots = draw_route_slots(jax.random.fold_in(seeds[6], 71), 0)
    saved_hidden = heavy_noise(seeds[4], (REPLICAS, EXP_WIN, SLOTS, HW), 0.036, 0.21582031, ((0, 8), (1, 4)), (0, 3, 8, 2.0))
    down_weight = noise(seeds[5], (EXP_WIN, HW, DW), HW ** -0.5, 0.21875, ((0, 4),))
    return dict(out_grad=out_grad, gates=gates, expert_ids=expert_ids, route_slots=route_slots, saved_hidden=saved_hidden, down_weight=down_weight)


def one_replica(out_grad, gates, expert_ids, route_slots, saved_hidden, down_weight):
    tok_index = jnp.arange(TOKENS, dtype=jnp.int32)
    source = tok_index // TOK_DEV
    valid = (expert_ids < EXP_WIN) & (route_slots >= 0)
    dump_row = EXP_WIN * SLOTS
    target = jnp.where(valid, expert_ids * SLOTS + source[:, None] * C_SRC + route_slots, dump_row).astype(jnp.int32)
    target_flat = target.reshape(-1)
    token_flat = jnp.broadcast_to(tok_index[:, None], (TOKENS, TOPK)).reshape(-1)
    row_token = jnp.full((dump_row + 1,), TOKENS, jnp.int32).at[target_flat].set(token_flat)[:-1]
    row_token = jnp.where(row_token == TOKENS, TOKENS, row_token).astype(jnp.int32)
    row_gate = jnp.zeros((dump_row + 1,), jnp.float32).at[target_flat].set(gates.reshape(-1).astype(jnp.float32))[:-1]
    padded = jnp.concatenate([out_grad, jnp.zeros((1, DW), out_grad.dtype)], axis=0)
    routed_grad = padded[row_token].reshape(EXP_WIN, SLOTS, DW)
    routed_gate = row_gate.reshape(EXP_WIN, SLOTS)
    routed_float = routed_grad.astype(jnp.float32)
    scaled_grad = (routed_gate[:, :, None] * routed_float).astype(jnp.bfloat16)
    weight_float = down_weight.astype(jnp.float32)
    hidden_float = saved_hidden.astype(jnp.float32)
    unit_grad = jnp.einsum("eqd,ehd->eqh", routed_float, weight_float)
    hidden_grad = (routed_gate[:, :, None] * unit_grad).astype(jnp.bfloat16)
    expert_out = jnp.einsum("eqh,ehd->eqd", hidden_float, weight_float)
    row_gate_grad = jnp.sum(routed_float * expert_out, axis=-1)
    flat_gate_grad = jnp.concatenate([row_gate_grad.reshape(-1), jnp.zeros((1,), jnp.float32)])
    gate_grad = flat_gate_grad[target]
    partial_value = jnp.einsum("eqh,eqd->ehd", hidden_float, scaled_grad.astype(jnp.float32)).astype(jnp.bfloat16)
    return hidden_grad, gate_grad, partial_value


def reference(out_grad, gates, expert_ids, route_slots, saved_hidden, down_weight):
    def step(total, inputs):
        grad_in, gate_in, ids_in, slots_in, hidden_in = inputs
        hidden_grad, gate_grad, partial_value = one_replica(grad_in, gate_in, ids_in, slots_in, hidden_in, down_weight)
        partial_value = lax.optimization_barrier(partial_value)
        return total + partial_value.astype(jnp.float32), (hidden_grad, gate_grad)

    start_total = jnp.zeros((EXP_WIN, HW, DW), jnp.float32)
    weight_grad, stacked = lax.scan(step, start_total, (out_grad, gates, expert_ids, route_slots, saved_hidden))
    return stacked[0], weight_grad, stacked[1]
```

```python
import functools
import math

import jax
import jax.numpy as jnp
from jax import lax
from jax.experimental import pallas as pl
from jax.experimental.pallas import tpu as pltpu
from jax.sharding import PartitionSpec as P

F32 = jnp.float32
BF16 = jnp.bfloat16
LIMIT = 60 * 1024 * 1024


def params(**kw):
    return pltpu.CompilerParams(vmem_limit_bytes=LIMIT, **kw)


def pad8(n):
    return -(-n // 8) * 8


def matmul_t(a, b, contract):
    return lax.dot_general(a, b, ((contract[:1], contract[1:]), ((), ())), preferred_element_type=F32)


def pack_kernel(experts, padded, ids_ref, slots_ref, gates_ref, grad_ref, *out_refs):
    me = lax.axis_index("expert")
    ids = ids_ref[...]
    slots = slots_ref[...]
    gates = gates_ref[...].astype(F32)
    valid = (ids < experts) & (slots >= 0)
    target = jnp.where(valid, (ids ^ me) * padded + slots, -1)
    row = lax.broadcasted_iota(jnp.int32, (experts * padded, ids.shape[1]), 0)
    chosen = jnp.zeros(row.shape, F32)
    for k in range(ids.shape[0]):
        chosen = jnp.where(row == target[k : k + 1, :], gates[k : k + 1, :], chosen)
    rows = jnp.dot(chosen.astype(BF16), grad_ref[...], preferred_element_type=F32)
    for k, out in enumerate(out_refs):
        out[...] = rows[k * padded : (k + 1) * padded, :].astype(BF16)


def pack(ids, slots, gates, grad, experts, padded):
    ranks, tokens = ids.shape
    width = grad.shape[1]
    steps = 4
    block = width // steps
    whole = pl.BlockSpec((ranks, tokens), lambda i: (0, 0))
    return pl.pallas_call(
        functools.partial(pack_kernel, experts, padded),
        grid=(steps,),
        in_specs=[whole, whole, whole, pl.BlockSpec((tokens, block), lambda i: (0, i))],
        out_specs=[pl.BlockSpec((padded, block), lambda i: (0, i))] * experts,
        out_shape=[jax.ShapeDtypeStruct((padded, width), BF16)] * experts,
        compiler_params=params(),
        name="pack",
    )(ids, slots, gates, grad)


def join_kernel(experts, capacity, *refs):
    blocks = refs[:experts]
    full_ref, own_ref, other_ref = refs[experts:]
    me = lax.axis_index("expert")
    core = lax.axis_index("dp") % 2
    slots = experts * capacity
    padded = blocks[0].shape[0]
    half = full_ref.shape[1] // 2
    total = jnp.zeros(full_ref.shape, F32)
    for k, block in enumerate(blocks):
        row = lax.broadcasted_iota(jnp.int32, (slots, padded), 0)
        col = lax.broadcasted_iota(jnp.int32, (slots, padded), 1)
        place = (row == (me ^ k) * capacity + col) & (col < capacity)
        total += jnp.dot(place.astype(BF16), block[...], preferred_element_type=F32)
    full_ref[...] = total.astype(BF16)
    own_ref[...] = full_ref[:, pl.ds(pl.multiple_of(core * half, 128), half)]
    other_ref[...] = full_ref[:, pl.ds(pl.multiple_of((1 - core) * half, 128), half)]


def join(blocks, capacity):
    experts = len(blocks)
    slots, width = experts * capacity, blocks[0].shape[1]
    vmem = pl.BlockSpec(memory_space=pltpu.VMEM)
    return pl.pallas_call(
        functools.partial(join_kernel, experts, capacity),
        in_specs=[vmem] * experts,
        out_specs=[vmem] * 3,
        out_shape=[
            jax.ShapeDtypeStruct((slots, width), BF16),
            jax.ShapeDtypeStruct((slots, width // 2), BF16),
            jax.ShapeDtypeStruct((slots, width // 2), BF16),
        ],
        compiler_params=params(),
        name="join",
    )(*blocks)


def hidden_kernel(full_ref, weight_ref, hidden_ref, grad_ref, row_ref, acc_ref):
    step = pl.program_id(0)
    unit = matmul_t(full_ref[...], weight_ref[...], (1, 1))
    grad_ref[...] = unit.astype(BF16)
    product = unit * hidden_ref[...].astype(F32)
    lanes = product[:, :128]
    for j in range(1, product.shape[1] // 128):
        lanes += product[:, j * 128 : (j + 1) * 128]

    @pl.when(step == 0)
    def _():
        acc_ref[...] = jnp.zeros_like(acc_ref)

    slots = lanes.shape[0]
    acc_ref[:slots, :] += lanes

    @pl.when(step == pl.num_programs(0) - 1)
    def _():
        row_ref[...] = jnp.sum(acc_ref[...].T, axis=0, keepdims=True)


def hidden_part(full, weight, hidden):
    slots, width = full.shape
    units = weight.shape[0]
    steps = 3
    block = units // steps
    lanes = -(-slots // 128) * 128
    return pl.pallas_call(
        hidden_kernel,
        grid=(steps,),
        in_specs=[
            pl.BlockSpec((slots, width), lambda i: (0, 0)),
            pl.BlockSpec((block, width), lambda i: (i, 0)),
            pl.BlockSpec((slots, block), lambda i: (0, i)),
        ],
        out_specs=[
            pl.BlockSpec((slots, block), lambda i: (0, i)),
            pl.BlockSpec((1, lanes), lambda i: (0, 0)),
        ],
        out_shape=[
            jax.ShapeDtypeStruct((slots, units), BF16),
            jax.ShapeDtypeStruct((1, lanes), F32),
        ],
        scratch_shapes=[pltpu.VMEM((lanes, 128), F32)],
        compiler_params=params(),
        name="hidden",
    )(full, weight, hidden)


def partial_kernel(side, count, *refs):
    hiddens, rows = refs[:count], refs[count : 2 * count]
    outs, total_ref = refs[2 * count : -1], refs[-1]
    index = lax.axis_index("dp")
    core = index % 2
    total = matmul_t(hiddens[0][...], rows[0][...], (0, 0))
    for hidden, row in zip(hiddens[1:], rows[1:]):
        total += matmul_t(hidden[...], row[...], (0, 0))
    total_ref[...] = total
    height = outs[0].shape[0]
    for out, mask in zip(outs, owner_masks(side)):
        owner = index ^ jnp.where(core == 0, mask[0], mask[1])
        start = pl.multiple_of(owner * height, 8)
        out[...] = total_ref[pl.ds(start, height), :].astype(out.dtype)


def partial(hiddens, rows, side, height):
    count = len(hiddens)
    units, half = hiddens[0].shape[1], rows[0].shape[1]
    slots = rows[0].shape[0]
    steps = 2
    block = half // steps
    masks = owner_masks(side)
    return pl.pallas_call(
        functools.partial(partial_kernel, side, count),
        grid=(steps,),
        in_specs=[pl.BlockSpec((slots, units), lambda i: (0, 0))] * count
        + [pl.BlockSpec((slots, block), lambda i: (0, i))] * count,
        out_specs=[pl.BlockSpec((height, block), lambda i: (0, i))] * len(masks),
        out_shape=[
            jax.ShapeDtypeStruct((height, half), F32 if n == 0 else BF16) for n in range(len(masks))
        ],
        scratch_shapes=[pltpu.VMEM((units, block), F32)],
        compiler_params=params(),
        name="partial",
    )(*hiddens, *rows)


def gather_masks(side):
    inner = [(d * 2) for d in range(1, side)]
    outer = [(d * side * 2) for d in range(1, side)]
    same = [(i, o) for i, o in zip(inner, outer)]
    cross = [(o ^ 1, i ^ 1) for i, o in zip(inner, outer)]
    return same, cross


def owner_masks(side):
    same = [(d * side * 2, d * 2) for d in range(1, side)]
    cross = [(a ^ 1, b ^ 1) for a, b in same]
    return [(0, 0), (1, 1)] + same + cross


def exchange(value, count, mask):
    pairs = [(i, i ^ mask[i % 2]) for i in range(count)]
    return lax.ppermute(value, "dp", pairs)


def total_kernel(terms, own_ref, *refs):
    own_terms, other_terms, out_ref = refs[:terms], refs[terms:-1], refs[-1]
    core = lax.axis_index("dp") % 2
    half = own_ref.shape[1]
    own = own_ref[...]
    for term in own_terms:
        own += term[...].astype(F32)
    other = other_terms[0][...].astype(F32)
    for term in other_terms[1:]:
        other += term[...].astype(F32)
    out_ref[:, pl.ds(pl.multiple_of(core * half, 128), half)] = own
    out_ref[:, pl.ds(pl.multiple_of((1 - core) * half, 128), half)] = other


def total(own, own_terms, other_terms):
    height, half = own.shape
    vmem = pl.BlockSpec(memory_space=pltpu.VMEM)
    return pl.pallas_call(
        functools.partial(total_kernel, len(own_terms)),
        in_specs=[vmem] * (1 + len(own_terms) + len(other_terms)),
        out_specs=vmem,
        out_shape=jax.ShapeDtypeStruct((height, 2 * half), F32),
        compiler_params=params(),
        name="total",
    )(own, *own_terms, *other_terms)


def gate_kernel(experts, capacity, *refs):
    tables = refs[:experts]
    ids_ref, slots_ref, gates_ref, out_ref = refs[experts:]
    me = lax.axis_index("expert")
    ids = ids_ref[...]
    slots = slots_ref[...]
    valid = (ids < experts) & (slots >= 0)
    target = jnp.where(valid, (ids ^ me) * capacity + slots, -1)
    value = jnp.zeros(ids.shape, F32)
    for k, table in enumerate(tables):
        for c in range(capacity):
            value = jnp.where(target == k * capacity + c, table[0, me * capacity + c], value)
    out_ref[...] = value / gates_ref[...].astype(F32)


def gate_part(tables, ids, slots, gates, capacity):
    experts = len(tables)
    vmem = pl.BlockSpec(memory_space=pltpu.VMEM)
    smem = pl.BlockSpec(memory_space=pltpu.SMEM)
    return pl.pallas_call(
        functools.partial(gate_kernel, experts, capacity),
        in_specs=[smem] * experts + [vmem] * 3,
        out_specs=vmem,
        out_shape=jax.ShapeDtypeStruct(ids.shape, F32),
        compiler_params=params(),
        name="gate",
    )(*tables, ids, slots, gates)


def on_device(out_grad, gates, expert_ids, route_slots, saved_hidden, down_weight):
    experts = lax.axis_size("expert")
    replicas = lax.axis_size("dp")
    side = math.isqrt(replicas // 2)
    assert 2 * side * side == replicas
    hidden = saved_hidden[0, 0]
    weight = down_weight[0]
    capacity = hidden.shape[0] // experts
    ids, slots, gate = expert_ids[0].T, route_slots[0].T, gates[0].T

    sent = pack(ids, slots, gate, out_grad[0], experts, pad8(capacity))
    blocks = [sent[0]]
    for k in range(1, experts):
        pairs = [(i, i ^ k) for i in range(experts)]
        blocks.append(lax.ppermute(sent[k], "expert", pairs))

    same, cross = gather_masks(side)
    hiddens = [hidden, exchange(hidden, replicas, (1, 1))]
    hiddens += [exchange(hidden, replicas, m) for m in same + cross]

    full, own, other = join(blocks, capacity)
    rows = [own, exchange(other, replicas, (1, 1))]
    rows += [exchange(own, replicas, m) for m in same]
    rows += [exchange(other, replicas, m) for m in cross]

    hidden_grad, row_sums = hidden_part(full, weight, hidden)
    tables = [row_sums]
    for k in range(1, experts):
        pairs = [(i, i ^ k) for i in range(experts)]
        tables.append(lax.ppermute(row_sums, "expert", pairs))

    height = hidden.shape[1] // replicas
    cut = partial(hiddens, rows, side, height)
    moved = [exchange(b, replicas, m) for b, m in zip(cut[1:], owner_masks(side)[1:])]
    weight_grad = total(cut[0], moved[1 : side], [moved[0]] + moved[side:])

    gate_grad = gate_part(tables, ids, slots, gate, capacity)
    return hidden_grad[None, None], weight_grad[None], gate_grad.T[None]


def solution(mesh):
    in_specs = (
        P("dp", "expert", None),
        P("dp", "expert", None),
        P("dp", "expert", None),
        P("dp", "expert", None),
        P("dp", "expert", None, None),
        P("expert", None, None),
    )
    out_specs = (P("dp", "expert", None, None), P("expert", "dp", None), P("dp", "expert", None))
    return jax.shard_map(
        on_device, mesh=mesh, in_specs=in_specs, out_specs=out_specs, check_vma=False
    )
```

```python
import functools
import math

import jax
import jax.numpy as jnp
from jax import lax
from jax.experimental import pallas as pl
from jax.experimental.pallas import tpu as pltpu
from jax.sharding import PartitionSpec as P


F32 = jnp.float32
BF16 = jnp.bfloat16
LIMIT = 24 * 1024 * 1024


def params(**kw):
    return pltpu.CompilerParams(vmem_limit_bytes=LIMIT, **kw)


def pad8(n):
    return -(-n // 8) * 8


def matmul_t(a, b, contract):
    return lax.dot_general(a, b, ((contract[:1], contract[1:]), ((), ())), preferred_element_type=F32)


def pack_kernel(experts, padded, ids_ref, slots_ref, gates_ref, grad_ref, *out_refs):
    me = lax.axis_index("expert")
    ids = ids_ref[...]
    slots = slots_ref[...]
    gates = gates_ref[...].astype(F32)
    valid = (ids < experts) & (slots >= 0)
    target = jnp.where(valid, (ids ^ me) * padded + slots, -1)
    row = lax.broadcasted_iota(jnp.int32, (experts * padded, ids.shape[1]), 0)
    chosen = jnp.zeros(row.shape, F32)
    for k in range(ids.shape[0]):
        chosen = jnp.where(row == target[k : k + 1, :], gates[k : k + 1, :], chosen)
    rows = jnp.dot(chosen.astype(BF16), grad_ref[...], preferred_element_type=F32)
    for k, out in enumerate(out_refs):
        out[...] = rows[k * padded : (k + 1) * padded, :].astype(BF16)


def pack(ids, slots, gates, grad, experts, padded):
    ranks, tokens = ids.shape
    width = grad.shape[1]
    steps = 4
    block = width // steps
    whole = pl.BlockSpec((ranks, tokens), lambda i: (0, 0))
    return pl.pallas_call(
        functools.partial(pack_kernel, experts, padded),
        grid=(steps,),
        in_specs=[whole, whole, whole, pl.BlockSpec((tokens, block), lambda i: (0, i))],
        out_specs=[pl.BlockSpec((padded, block), lambda i: (0, i))] * experts,
        out_shape=[jax.ShapeDtypeStruct((padded, width), BF16)] * experts,
        compiler_params=params(),
        name="pack",
    )(ids, slots, gates, grad)


def join_kernel(experts, capacity, *refs):
    blocks = refs[:experts]
    full_ref, own_ref, other_ref = refs[experts:]
    me = lax.axis_index("expert")
    core = lax.axis_index("dp") % 2
    slots = experts * capacity
    padded = blocks[0].shape[0]
    half = full_ref.shape[1] // 2
    total = jnp.zeros(full_ref.shape, F32)
    for k, block in enumerate(blocks):
        row = lax.broadcasted_iota(jnp.int32, (slots, padded), 0)
        col = lax.broadcasted_iota(jnp.int32, (slots, padded), 1)
        place = (row == (me ^ k) * capacity + col) & (col < capacity)
        total += jnp.dot(place.astype(BF16), block[...], preferred_element_type=F32)
    full_ref[...] = total.astype(BF16)
    own_ref[...] = full_ref[:, pl.ds(pl.multiple_of(core * half, 128), half)]
    other_ref[...] = full_ref[:, pl.ds(pl.multiple_of((1 - core) * half, 128), half)]


def join(blocks, capacity):
    experts = len(blocks)
    slots, width = experts * capacity, blocks[0].shape[1]
    vmem = pl.BlockSpec(memory_space=pltpu.VMEM)
    return pl.pallas_call(
        functools.partial(join_kernel, experts, capacity),
        in_specs=[vmem] * experts,
        out_specs=[vmem] * 3,
        out_shape=[
            jax.ShapeDtypeStruct((slots, width), BF16),
            jax.ShapeDtypeStruct((slots, width // 2), BF16),
            jax.ShapeDtypeStruct((slots, width // 2), BF16),
        ],
        compiler_params=params(),
        name="join",
    )(*blocks)


def hidden_kernel(full_ref, weight_ref, hidden_ref, grad_ref, row_ref, acc_ref):
    step = pl.program_id(0)
    unit = matmul_t(full_ref[...], weight_ref[...], (1, 1))
    grad_ref[...] = unit.astype(BF16)
    product = unit * hidden_ref[...].astype(F32)
    lanes = product[:, :128]
    for j in range(1, product.shape[1] // 128):
        lanes += product[:, j * 128 : (j + 1) * 128]

    @pl.when(step == 0)
    def _():
        acc_ref[...] = jnp.zeros_like(acc_ref)

    slots = lanes.shape[0]
    acc_ref[:slots, :] += lanes

    @pl.when(step == pl.num_programs(0) - 1)
    def _():
        row_ref[...] = jnp.sum(acc_ref[...].T, axis=0, keepdims=True)


def hidden_part(full, weight, hidden):
    slots, width = full.shape
    units = weight.shape[0]
    steps = 3
    block = units // steps
    lanes = -(-slots // 128) * 128
    return pl.pallas_call(
        hidden_kernel,
        grid=(steps,),
        in_specs=[
            pl.BlockSpec((slots, width), lambda i: (0, 0)),
            pl.BlockSpec((block, width), lambda i: (i, 0)),
            pl.BlockSpec((slots, block), lambda i: (0, i)),
        ],
        out_specs=[
            pl.BlockSpec((slots, block), lambda i: (0, i)),
            pl.BlockSpec((1, lanes), lambda i: (0, 0)),
        ],
        out_shape=[
            jax.ShapeDtypeStruct((slots, units), BF16),
            jax.ShapeDtypeStruct((1, lanes), F32),
        ],
        scratch_shapes=[pltpu.VMEM((lanes, 128), F32)],
        compiler_params=params(),
        name="hidden",
    )(full, weight, hidden)


def partial_kernel(side, count, *refs):
    hiddens, rows = refs[:count], refs[count : 2 * count]
    outs, total_ref = refs[2 * count : -1], refs[-1]
    index = lax.axis_index("dp")
    core = index % 2
    total = matmul_t(hiddens[0][...], rows[0][...], (0, 0))
    for hidden, row in zip(hiddens[1:], rows[1:]):
        total += matmul_t(hidden[...], row[...], (0, 0))
    total_ref[...] = total
    height = outs[0].shape[0]
    for out, mask in zip(outs, owner_masks(side)):
        owner = index ^ jnp.where(core == 0, mask[0], mask[1])
        start = pl.multiple_of(owner * height, 8)
        out[...] = total_ref[pl.ds(start, height), :].astype(out.dtype)


def partial(hiddens, rows, side, height):
    count = len(hiddens)
    units, half = hiddens[0].shape[1], rows[0].shape[1]
    slots = rows[0].shape[0]
    steps = 2
    block = half // steps
    masks = owner_masks(side)
    return pl.pallas_call(
        functools.partial(partial_kernel, side, count),
        grid=(steps,),
        in_specs=[pl.BlockSpec((slots, units), lambda i: (0, 0))] * count
        + [pl.BlockSpec((slots, block), lambda i: (0, i))] * count,
        out_specs=[pl.BlockSpec((height, block), lambda i: (0, i))] * len(masks),
        out_shape=[
            jax.ShapeDtypeStruct((height, half), F32 if n == 0 else BF16) for n in range(len(masks))
        ],
        scratch_shapes=[pltpu.VMEM((units, block), F32)],
        compiler_params=params(),
        name="partial",
    )(*hiddens, *rows)


def gather_masks(side):
    inner = [(d * 2) for d in range(1, side)]
    outer = [(d * side * 2) for d in range(1, side)]
    same = [(i, o) for i, o in zip(inner, outer)]
    cross = [(o ^ 1, i ^ 1) for i, o in zip(inner, outer)]
    return same, cross


def owner_masks(side):
    same = [(d * side * 2, d * 2) for d in range(1, side)]
    cross = [(a ^ 1, b ^ 1) for a, b in same]
    return [(0, 0), (1, 1)] + same + cross


def exchange(value, count, mask):
    pairs = [(i, i ^ mask[i % 2]) for i in range(count)]
    return lax.ppermute(value, "dp", pairs)


def total_kernel(terms, own_ref, *refs):
    own_terms, other_terms, out_ref = refs[:terms], refs[terms:-1], refs[-1]
    core = lax.axis_index("dp") % 2
    half = own_ref.shape[1]
    own = own_ref[...]
    for term in own_terms:
        own += term[...].astype(F32)
    other = other_terms[0][...].astype(F32)
    for term in other_terms[1:]:
        other += term[...].astype(F32)
    out_ref[:, pl.ds(pl.multiple_of(core * half, 128), half)] = own
    out_ref[:, pl.ds(pl.multiple_of((1 - core) * half, 128), half)] = other


def total(own, own_terms, other_terms):
    height, half = own.shape
    vmem = pl.BlockSpec(memory_space=pltpu.VMEM)
    return pl.pallas_call(
        functools.partial(total_kernel, len(own_terms)),
        in_specs=[vmem] * (1 + len(own_terms) + len(other_terms)),
        out_specs=vmem,
        out_shape=jax.ShapeDtypeStruct((height, 2 * half), F32),
        compiler_params=params(),
        name="total",
    )(own, *own_terms, *other_terms)


def gate_kernel(experts, capacity, *refs):
    tables = refs[:experts]
    ids_ref, slots_ref, gates_ref, out_ref = refs[experts:]
    me = lax.axis_index("expert")
    ids = ids_ref[...]
    slots = slots_ref[...]
    valid = (ids < experts) & (slots >= 0)
    target = jnp.where(valid, (ids ^ me) * capacity + slots, -1)
    value = jnp.zeros(ids.shape, F32)
    for k, table in enumerate(tables):
        for c in range(capacity):
            value = jnp.where(target == k * capacity + c, table[0, me * capacity + c], value)
    out_ref[...] = value / gates_ref[...].astype(F32)


def gate_part(tables, ids, slots, gates, capacity):
    experts = len(tables)
    vmem = pl.BlockSpec(memory_space=pltpu.VMEM)
    smem = pl.BlockSpec(memory_space=pltpu.SMEM)
    return pl.pallas_call(
        functools.partial(gate_kernel, experts, capacity),
        in_specs=[smem] * experts + [vmem] * 3,
        out_specs=vmem,
        out_shape=jax.ShapeDtypeStruct(ids.shape, F32),
        compiler_params=params(),
        name="gate",
    )(*tables, ids, slots, gates)


def on_device(out_grad, gates, expert_ids, route_slots, saved_hidden, down_weight):
    experts = lax.axis_size("expert")
    replicas = lax.axis_size("dp")
    side = math.isqrt(replicas // 2)
    assert 2 * side * side == replicas
    hidden = saved_hidden[0, 0]
    weight = down_weight[0]
    capacity = hidden.shape[0] // experts
    ids, slots, gate = expert_ids[0].T, route_slots[0].T, gates[0].T

    sent = pack(ids, slots, gate, out_grad[0], experts, pad8(capacity))
    blocks = [sent[0]]
    for k in range(1, experts):
        pairs = [(i, i ^ k) for i in range(experts)]
        blocks.append(lax.ppermute(sent[k], "expert", pairs))

    same, cross = gather_masks(side)
    routes = [(1, 1)] + same + cross
    hiddens = [hidden]
    for mask in routes:
        hiddens.append(exchange(hidden, replicas, mask))

    blocks, hiddens = lax.optimization_barrier((blocks, hiddens))
    full, own, other = join(blocks, capacity)
    rows = [own]
    for mask in routes:
        rows.append(exchange(own if mask in same else other, replicas, mask))

    hidden_grad, row_sums = hidden_part(full, weight, hidden)
    tables = [row_sums]
    for k in range(1, experts):
        pairs = [(i, i ^ k) for i in range(experts)]
        tables.append(lax.ppermute(row_sums, "expert", pairs))

    height = hidden.shape[1] // replicas
    cut = partial(hiddens, rows, side, height)
    moved = []
    for n, mask in enumerate(owner_masks(side)[1:]):
        moved.append(exchange(cut[n + 1], replicas, mask))
    weight_grad = total(cut[0], moved[1:side], [moved[0]] + moved[side:])

    gate_grad = gate_part(tables, ids, slots, gate, capacity)
    return hidden_grad[None, None], weight_grad[None], gate_grad.T[None]


def solution(mesh):
    in_specs = (
        P("dp", "expert", None),
        P("dp", "expert", None),
        P("dp", "expert", None),
        P("dp", "expert", None),
        P("dp", "expert", None, None),
        P("expert", None, None),
    )
    out_specs = (P("dp", "expert", None, None), P("expert", "dp", None), P("dp", "expert", None))
    return jax.shard_map(
        on_device, mesh=mesh, in_specs=in_specs, out_specs=out_specs, check_vma=False
    )
```

```python
import functools
import math

import jax
import jax.numpy as jnp
from jax import lax
from jax.experimental import pallas as pl
from jax.experimental.pallas import tpu as pltpu
from jax.sharding import PartitionSpec as P


F32 = jnp.float32
BF16 = jnp.bfloat16
LIMIT = 24 * 1024 * 1024


def params(**kw):
    return pltpu.CompilerParams(vmem_limit_bytes=LIMIT, **kw)


def in_hbm(x):
    return pltpu.with_memory_space_constraint(x, pltpu.HBM)


def pad8(n):
    return -(-n // 8) * 8


def matmul_t(a, b, contract):
    return lax.dot_general(a, b, ((contract[:1], contract[1:]), ((), ())), preferred_element_type=F32)


def pack_kernel(experts, padded, pieces, *refs):
    arrays, out_refs = refs[:4], refs[4 : 4 + experts]
    ids_ref, slots_ref, gates_ref, grad_ref, small_sems, grad_sems = refs[4 + experts :]
    small = [
        pltpu.make_async_copy(src, dst, small_sems.at[n])
        for n, (src, dst) in enumerate(zip(arrays[:3], (ids_ref, slots_ref, gates_ref)))
    ]
    for copy in small:
        copy.start()
    width = grad_ref.shape[1] // pieces
    large = []
    for n in range(pieces):
        columns = pl.ds(n * width, width)
        large.append(
            pltpu.make_async_copy(arrays[3].at[:, columns], grad_ref.at[:, columns], grad_sems.at[n])
        )
        large[-1].start()
    for copy in small:
        copy.wait()
    me = lax.axis_index("expert")
    ids = ids_ref[...]
    slots = slots_ref[...]
    gates = gates_ref[...].astype(F32)
    valid = (ids < experts) & (slots >= 0)
    target = jnp.where(valid, (ids ^ me) * padded + slots, -1)
    row = lax.broadcasted_iota(jnp.int32, (experts * padded, ids.shape[1]), 0)
    chosen = jnp.zeros(row.shape, F32)
    for k in range(ids.shape[0]):
        chosen = jnp.where(row == target[k : k + 1, :], gates[k : k + 1, :], chosen)
    chosen = chosen.astype(BF16)
    for n in range(pieces):
        columns = slice(n * width, (n + 1) * width)
        large[n].wait()
        rows = jnp.dot(chosen, grad_ref[:, columns], preferred_element_type=F32)
        for k, out in enumerate(out_refs):
            out[:, columns] = rows[k * padded : (k + 1) * padded, :].astype(BF16)


def pack(ids, slots, gates, grad, experts, padded):
    width = grad.shape[1]
    pieces = 4
    arrays = (ids, slots, gates, grad)
    return pl.pallas_call(
        functools.partial(pack_kernel, experts, padded, pieces),
        in_specs=[pl.BlockSpec(memory_space=pltpu.HBM)] * 4,
        out_specs=[pl.BlockSpec(memory_space=pltpu.VMEM)] * experts,
        out_shape=[jax.ShapeDtypeStruct((padded, width), BF16)] * experts,
        scratch_shapes=[pltpu.VMEM(a.shape, a.dtype) for a in arrays]
        + [pltpu.SemaphoreType.DMA((3,)), pltpu.SemaphoreType.DMA((pieces,))],
        compiler_params=params(),
        name="pack",
    )(*map(in_hbm, arrays))


def join_kernel(experts, capacity, *refs):
    blocks = refs[:experts]
    full_ref, own_ref, other_ref = refs[experts:]
    me = lax.axis_index("expert")
    core = lax.axis_index("dp") % 2
    slots = experts * capacity
    padded = blocks[0].shape[0]
    half = full_ref.shape[1] // 2
    total = jnp.zeros(full_ref.shape, F32)
    for k, block in enumerate(blocks):
        row = lax.broadcasted_iota(jnp.int32, (slots, padded), 0)
        col = lax.broadcasted_iota(jnp.int32, (slots, padded), 1)
        place = (row == (me ^ k) * capacity + col) & (col < capacity)
        total += jnp.dot(place.astype(BF16), block[...], preferred_element_type=F32)
    full_ref[...] = total.astype(BF16)
    own_ref[...] = full_ref[:, pl.ds(pl.multiple_of(core * half, 128), half)]
    other_ref[...] = full_ref[:, pl.ds(pl.multiple_of((1 - core) * half, 128), half)]


def join(blocks, capacity):
    experts = len(blocks)
    slots, width = experts * capacity, blocks[0].shape[1]
    vmem = pl.BlockSpec(memory_space=pltpu.VMEM)
    return pl.pallas_call(
        functools.partial(join_kernel, experts, capacity),
        in_specs=[vmem] * experts,
        out_specs=[vmem] * 3,
        out_shape=[
            jax.ShapeDtypeStruct((slots, width), BF16),
            jax.ShapeDtypeStruct((slots, width // 2), BF16),
            jax.ShapeDtypeStruct((slots, width // 2), BF16),
        ],
        compiler_params=params(),
        name="join",
    )(*blocks)


def load_kernel(weight_hbm, hidden_hbm, weight_ref, hidden_ref, sems):
    copies = [
        pltpu.make_async_copy(weight_hbm, weight_ref, sems.at[0]),
        pltpu.make_async_copy(hidden_hbm, hidden_ref, sems.at[1]),
    ]
    for copy in copies:
        copy.start()
    for copy in copies:
        copy.wait()


def load(weight, hidden):
    return pl.pallas_call(
        load_kernel,
        in_specs=[pl.BlockSpec(memory_space=pltpu.HBM)] * 2,
        out_specs=[pl.BlockSpec(memory_space=pltpu.VMEM)] * 2,
        out_shape=[jax.ShapeDtypeStruct(a.shape, a.dtype) for a in (weight, hidden)],
        scratch_shapes=[pltpu.SemaphoreType.DMA((2,))],
        compiler_params=params(),
        name="load",
    )(in_hbm(weight), in_hbm(hidden))


def stack_kernel(side, count, depth, *refs):
    hiddens, (left_ref, stack_ref, turned_ref) = refs[:count], refs[count:]
    slots = hiddens[0].shape[0]
    for n, hidden in enumerate(hiddens):
        stack_ref[n * depth : n * depth + slots, :] = hidden[...].astype(F32)
        if slots < depth:
            stack_ref[n * depth + slots : (n + 1) * depth, :] = jnp.zeros(
                (depth - slots, stack_ref.shape[1]), F32
            )
    turned_ref[...] = stack_ref[...].T
    index = lax.axis_index("dp")
    masks = owner_masks(side)
    height = left_ref.shape[0] // len(masks)
    for n, mask in enumerate(masks):
        owner = index ^ jnp.where(index % 2 == 0, mask[0], mask[1])
        start = pl.multiple_of(owner * height, 8)
        left_ref[n * height : (n + 1) * height, :] = turned_ref[pl.ds(start, height), :].astype(BF16)


def stack(hiddens, side, depth, height):
    count = len(hiddens)
    units = hiddens[0].shape[1]
    vmem = pl.BlockSpec(memory_space=pltpu.VMEM)
    return pl.pallas_call(
        functools.partial(stack_kernel, side, count, depth),
        in_specs=[vmem] * count,
        out_specs=vmem,
        out_shape=jax.ShapeDtypeStruct((2 * side * height, count * depth), BF16),
        scratch_shapes=[
            pltpu.VMEM((count * depth, units), F32),
            pltpu.VMEM((units, count * depth), F32),
        ],
        compiler_params=params(),
        name="stack",
    )(*hiddens)


def unit_kernel(capacity, full_ref, weight_ref, hidden_ref, grad_ref, *refs):
    tables, sums_ref = refs[:-1], refs[-1]
    me = lax.axis_index("expert")
    unit = matmul_t(full_ref[...], weight_ref[...], (1, 1))
    grad_ref[...] = unit.astype(BF16)
    sums = jnp.sum(unit * hidden_ref[...].astype(F32), axis=1, keepdims=True)
    sums_ref[...] = jnp.zeros_like(sums_ref)
    sums_ref[: sums.shape[0], :] = jnp.broadcast_to(sums, (sums.shape[0], sums_ref.shape[1]))
    for k, table in enumerate(tables):
        table[...] = sums_ref[pl.ds((me ^ k) * capacity, table.shape[0]), :]


def unit_part(full, weight, hidden, experts):
    slots, _ = full.shape
    units = weight.shape[0]
    capacity = slots // experts
    vmem = pl.BlockSpec(memory_space=pltpu.VMEM)
    return pl.pallas_call(
        functools.partial(unit_kernel, capacity),
        in_specs=[vmem] * 3,
        out_specs=[vmem] * (1 + experts),
        out_shape=[jax.ShapeDtypeStruct((slots, units), BF16)]
        + [jax.ShapeDtypeStruct((pad8(capacity), 128), F32)] * experts,
        scratch_shapes=[pltpu.VMEM((pad8(slots) + 8, 128), F32)],
        compiler_params=params(),
        name="unit",
    )(full, weight, hidden)


def partial_kernel(depth, left_ref, *refs):
    masks = (len(refs) - 1) // 2
    rows, outs, right_ref = refs[:masks], refs[masks : 2 * masks], refs[-1]
    slots = rows[0].shape[0]
    for n, row in enumerate(rows):
        right_ref[n * depth : n * depth + slots, :] = row[...]
        if slots < depth:
            right_ref[n * depth + slots : (n + 1) * depth, :] = jnp.zeros(
                (depth - slots, right_ref.shape[1]), BF16
            )
    height = outs[0].shape[0]
    total = jnp.dot(left_ref[...], right_ref[...], preferred_element_type=F32)
    for n, out in enumerate(outs):
        out[...] = total[n * height : (n + 1) * height, :].astype(out.dtype)


def partial(left, rows, depth):
    count = len(rows)
    half = rows[0].shape[1]
    height = left.shape[0] // count
    vmem = pl.BlockSpec(memory_space=pltpu.VMEM)
    return pl.pallas_call(
        functools.partial(partial_kernel, depth),
        in_specs=[vmem] * (1 + count),
        out_specs=[vmem] * count,
        out_shape=[jax.ShapeDtypeStruct((height, half), F32 if n == 0 else BF16) for n in range(count)],
        scratch_shapes=[pltpu.VMEM((count * depth, half), BF16)],
        compiler_params=params(),
        name="partial",
    )(left, *rows)


def gather_masks(side):
    inner = [(d * 2) for d in range(1, side)]
    outer = [(d * side * 2) for d in range(1, side)]
    same = [(i, o) for i, o in zip(inner, outer)]
    cross = [(o ^ 1, i ^ 1) for i, o in zip(inner, outer)]
    return same, cross


def owner_masks(side):
    same = [(d * side * 2, d * 2) for d in range(1, side)]
    cross = [(a ^ 1, b ^ 1) for a, b in same]
    return [(0, 0), (1, 1)] + same + cross


def exchange(value, count, mask):
    pairs = [(i, i ^ mask[i % 2]) for i in range(count)]
    return lax.ppermute(value, "dp", pairs)


def total_kernel(terms, own_ref, *refs):
    own_terms, other_terms, out_ref = refs[:terms], refs[terms:-1], refs[-1]
    core = lax.axis_index("dp") % 2
    half = own_ref.shape[1]
    own = own_ref[...]
    for term in own_terms:
        own += term[...].astype(F32)
    other = other_terms[0][...].astype(F32)
    for term in other_terms[1:]:
        other += term[...].astype(F32)
    out_ref[:, pl.ds(pl.multiple_of(core * half, 128), half)] = own
    out_ref[:, pl.ds(pl.multiple_of((1 - core) * half, 128), half)] = other


def total(own, own_terms, other_terms):
    height, half = own.shape
    vmem = pl.BlockSpec(memory_space=pltpu.VMEM)
    return pl.pallas_call(
        functools.partial(total_kernel, len(own_terms)),
        in_specs=[vmem] * (1 + len(own_terms) + len(other_terms)),
        out_specs=vmem,
        out_shape=jax.ShapeDtypeStruct((height, 2 * half), F32),
        compiler_params=params(),
        name="total",
    )(own, *own_terms, *other_terms)


def gate_kernel(experts, *refs):
    tables = refs[:experts]
    ids_ref, slots_ref, gates_ref, out_ref = refs[experts:]
    me = lax.axis_index("expert")
    padded, lanes = tables[0].shape
    ids = ids_ref[...]
    slots = slots_ref[...]
    gates = gates_ref[...].astype(F32)
    valid = (ids < experts) & (slots >= 0)
    target = jnp.where(valid, (ids ^ me) * padded + slots, -1)
    column = jnp.concatenate([table[...] for table in tables], axis=0)
    row = lax.broadcasted_iota(jnp.int32, column.shape, 0)
    for c in range(0, ids.shape[1], lanes):
        found = [
            jnp.sum(jnp.where(row == target[k : k + 1, c : c + lanes], column, 0.0), axis=0, keepdims=True)
            for k in range(ids.shape[0])
        ]
        out_ref[:, c : c + lanes] = jnp.concatenate(found, axis=0) / gates[:, c : c + lanes]


def gate_part(tables, ids, slots, gates):
    experts = len(tables)
    vmem = pl.BlockSpec(memory_space=pltpu.VMEM)
    return pl.pallas_call(
        functools.partial(gate_kernel, experts),
        in_specs=[vmem] * (experts + 3),
        out_specs=vmem,
        out_shape=jax.ShapeDtypeStruct(ids.shape, F32),
        compiler_params=params(),
        name="gate",
    )(*tables, ids, slots, gates)


def on_device(out_grad, gates, expert_ids, route_slots, saved_hidden, down_weight):
    experts = lax.axis_size("expert")
    replicas = lax.axis_size("dp")
    side = math.isqrt(replicas // 2)
    assert 2 * side * side == replicas
    hidden = saved_hidden[0, 0]
    weight = down_weight[0]
    capacity = hidden.shape[0] // experts
    ids, slots, gate = expert_ids[0].T, route_slots[0].T, gates[0].T

    sent = pack(ids, slots, gate, out_grad[0], experts, pad8(capacity))
    blocks = [sent[0]]
    for k in range(1, experts):
        pairs = [(i, i ^ k) for i in range(experts)]
        blocks.append(lax.ppermute(sent[k], "expert", pairs))

    same, cross = gather_masks(side)
    routes = [(1, 1)] + same + cross
    moved_hiddens = []
    for mask in routes:
        moved_hiddens.append(exchange(hidden, replicas, mask))

    depth = -(-hidden.shape[0] // 32) * 32
    height = hidden.shape[1] // replicas
    weight, hidden = load(weight, hidden)
    left = stack([hidden] + moved_hiddens, side, depth, height)
    full, own, other = join(blocks, capacity)
    rows = [own]
    for mask in routes:
        rows.append(exchange(own if mask in same else other, replicas, mask))

    hidden_grad, *sums = unit_part(full, weight, hidden, experts)
    tables = [sums[0]]
    for k in range(1, experts):
        pairs = [(i, i ^ k) for i in range(experts)]
        tables.append(lax.ppermute(sums[k], "expert", pairs))

    cut = partial(left, rows, depth)
    moved = []
    for n, mask in enumerate(owner_masks(side)[1:]):
        moved.append(exchange(cut[n + 1], replicas, mask))
    weight_grad = total(cut[0], moved[1:side], [moved[0]] + moved[side:])

    gate_grad = gate_part(tables, ids, slots, gate)
    return hidden_grad[None, None], weight_grad[None], gate_grad.T[None]


def solution(mesh):
    in_specs = (
        P("dp", "expert", None),
        P("dp", "expert", None),
        P("dp", "expert", None),
        P("dp", "expert", None),
        P("dp", "expert", None, None),
        P("expert", None, None),
    )
    out_specs = (P("dp", "expert", None, None), P("expert", "dp", None), P("dp", "expert", None))
    return jax.shard_map(
        on_device, mesh=mesh, in_specs=in_specs, out_specs=out_specs, check_vma=False
    )
```

```python
import functools
import math

import jax
import jax.numpy as jnp
from jax import lax
from jax.experimental import pallas as pl
from jax.experimental.pallas import tpu as pltpu
from jax.sharding import PartitionSpec as P


F32 = jnp.float32
BF16 = jnp.bfloat16
LIMIT = 24 * 1024 * 1024


def params(**kw):
    return pltpu.CompilerParams(vmem_limit_bytes=LIMIT, **kw)


def in_hbm(x):
    return pltpu.with_memory_space_constraint(x, pltpu.HBM)


def pad8(n):
    return -(-n // 8) * 8


def matmul_t(a, b, contract):
    return lax.dot_general(a, b, ((contract[:1], contract[1:]), ((), ())), preferred_element_type=F32)


def pack_kernel(experts, padded, pieces, *refs):
    arrays, out_refs = refs[:4], refs[4 : 4 + experts]
    ids_ref, slots_ref, gates_ref, grad_ref, small_sems, grad_sems = refs[4 + experts :]
    small = [
        pltpu.make_async_copy(src, dst, small_sems.at[n])
        for n, (src, dst) in enumerate(zip(arrays[:3], (ids_ref, slots_ref, gates_ref)))
    ]
    for copy in small:
        copy.start()
    width = grad_ref.shape[1] // pieces
    large = []
    for n in range(pieces):
        columns = pl.ds(n * width, width)
        large.append(
            pltpu.make_async_copy(arrays[3].at[:, columns], grad_ref.at[:, columns], grad_sems.at[n])
        )
        large[-1].start()
    for copy in small:
        copy.wait()
    me = lax.axis_index("expert")
    ids = ids_ref[...]
    slots = slots_ref[...]
    gates = gates_ref[...].astype(F32)
    valid = (ids < experts) & (slots >= 0)
    target = jnp.where(valid, (ids ^ me) * padded + slots, -1)
    row = lax.broadcasted_iota(jnp.int32, (experts * padded, ids.shape[1]), 0)
    chosen = jnp.zeros(row.shape, F32)
    for k in range(ids.shape[0]):
        chosen = jnp.where(row == target[k : k + 1, :], gates[k : k + 1, :], chosen)
    chosen = chosen.astype(BF16)
    for n in range(pieces):
        columns = slice(n * width, (n + 1) * width)
        large[n].wait()
        rows = jnp.dot(chosen, grad_ref[:, columns], preferred_element_type=F32)
        for k, out in enumerate(out_refs):
            out[:, columns] = rows[k * padded : (k + 1) * padded, :].astype(BF16)


def pack(ids, slots, gates, grad, experts, padded):
    width = grad.shape[1]
    pieces = 4
    arrays = (ids, slots, gates, grad)
    return pl.pallas_call(
        functools.partial(pack_kernel, experts, padded, pieces),
        in_specs=[pl.BlockSpec(memory_space=pltpu.HBM)] * 4,
        out_specs=[pl.BlockSpec(memory_space=pltpu.VMEM)] * experts,
        out_shape=[jax.ShapeDtypeStruct((padded, width), BF16)] * experts,
        scratch_shapes=[pltpu.VMEM(a.shape, a.dtype) for a in arrays]
        + [pltpu.SemaphoreType.DMA((3,)), pltpu.SemaphoreType.DMA((pieces,))],
        compiler_params=params(),
        name="pack",
    )(*map(in_hbm, arrays))


def rows_of(block, row_of_first, rows, capacity):
    padded = block.shape[0]
    row = lax.broadcasted_iota(jnp.int32, (rows, padded), 0)
    col = lax.broadcasted_iota(jnp.int32, (rows, padded), 1)
    place = (row == row_of_first + col) & (col < capacity)
    return jnp.dot(place.astype(BF16), block[...], preferred_element_type=F32)


def store_halves(rows, part_ref, own_ref, other_ref):
    core = lax.axis_index("dp") % 2
    half = own_ref.shape[1]
    part_ref[...] = rows.astype(BF16)
    own_ref[...] = part_ref[:, pl.ds(pl.multiple_of(core * half, 128), half)]
    other_ref[...] = part_ref[:, pl.ds(pl.multiple_of((1 - core) * half, 128), half)]


def join_kernel(first, capacity, *refs):
    count = len(refs) - 3
    me = lax.axis_index("expert")
    part_ref, own_ref, other_ref = refs[count:]
    rows = part_ref.shape[0]
    total = jnp.zeros(part_ref.shape, F32)
    for k, block in enumerate(refs[:count]):
        total += rows_of(block, ((me ^ (first + k)) % count) * capacity, rows, capacity)
    store_halves(total, part_ref, own_ref, other_ref)


def join(blocks, first, capacity):
    rows, width = len(blocks) * capacity, blocks[0].shape[1]
    vmem = pl.BlockSpec(memory_space=pltpu.VMEM)
    return pl.pallas_call(
        functools.partial(join_kernel, first, capacity),
        in_specs=[vmem] * len(blocks),
        out_specs=[vmem] * 3,
        out_shape=[jax.ShapeDtypeStruct((rows, w), BF16) for w in (width, width // 2, width // 2)],
        compiler_params=params(),
        name="join",
    )(*blocks)


def load_kernel(weight_hbm, hidden_hbm, weight_ref, hidden_ref, sems):
    copies = [
        pltpu.make_async_copy(weight_hbm, weight_ref, sems.at[0]),
        pltpu.make_async_copy(hidden_hbm, hidden_ref, sems.at[1]),
    ]
    for copy in copies:
        copy.start()
    for copy in copies:
        copy.wait()


def load(weight, hidden):
    return pl.pallas_call(
        load_kernel,
        in_specs=[pl.BlockSpec(memory_space=pltpu.HBM)] * 2,
        out_specs=[pl.BlockSpec(memory_space=pltpu.VMEM)] * 2,
        out_shape=[jax.ShapeDtypeStruct(a.shape, a.dtype) for a in (weight, hidden)],
        scratch_shapes=[pltpu.SemaphoreType.DMA((2,))],
        compiler_params=params(),
        name="load",
    )(in_hbm(weight), in_hbm(hidden))


def stack_kernel(side, count, depth, *refs):
    hiddens, (left_ref, stack_ref, turned_ref) = refs[:count], refs[count:]
    slots, units = hiddens[0].shape
    rows = slots // 2
    upper = lax.axis_index("expert") // (lax.axis_size("expert") // 2)
    for n, hidden in enumerate(hiddens):
        values = hidden[...].astype(F32)
        lower, higher = values[:rows, :], values[rows:, :]
        for part in range(2):
            at = (2 * n + part) * depth
            stack_ref[at : at + rows, :] = jnp.where(upper == part, lower, higher)
            if rows < depth:
                stack_ref[at + rows : at + depth, :] = jnp.zeros((depth - rows, units), F32)
    turned_ref[...] = stack_ref[...].T
    index = lax.axis_index("dp")
    masks = owner_masks(side)
    height = left_ref.shape[0] // len(masks)
    for n, mask in enumerate(masks):
        owner = index ^ jnp.where(index % 2 == 0, mask[0], mask[1])
        start = pl.multiple_of(owner * height, 8)
        left_ref[n * height : (n + 1) * height, :] = turned_ref[pl.ds(start, height), :].astype(BF16)


def stack(hiddens, side, depth, height):
    count = len(hiddens)
    _, units = hiddens[0].shape
    vmem = pl.BlockSpec(memory_space=pltpu.VMEM)
    return pl.pallas_call(
        functools.partial(stack_kernel, side, count, depth),
        in_specs=[vmem] * count,
        out_specs=vmem,
        out_shape=jax.ShapeDtypeStruct((2 * side * height, 2 * count * depth), BF16),
        scratch_shapes=[
            pltpu.VMEM((2 * count * depth, units), F32),
            pltpu.VMEM((units, 2 * count * depth), F32),
        ],
        compiler_params=params(),
        name="stack",
    )(*hiddens)


def unit_kernel(experts, capacity, near_ref, far_ref, weight_ref, hidden_ref, *refs):
    grad_ref, kept_ref, sent_ref, full_ref, sums_ref = refs
    me = lax.axis_index("expert")
    rows = near_ref.shape[0]
    lower = me // (experts // 2) == 0
    near = near_ref[...]
    far = far_ref[...]
    full_ref[:rows, :] = jnp.where(lower, near, far)
    full_ref[rows : 2 * rows, :] = jnp.where(lower, far, near)
    unit = matmul_t(full_ref[...], weight_ref[...], (1, 1))
    grad_ref[...] = unit.astype(BF16)
    sums = jnp.sum(unit * hidden_ref[...].astype(F32), axis=1, keepdims=True)
    sums_ref[...] = jnp.zeros_like(sums_ref)
    sums_ref[: sums.shape[0], :] = jnp.broadcast_to(sums, (sums.shape[0], sums_ref.shape[1]))
    padded = pad8(capacity)
    for k in range(experts):
        out = sent_ref if k % 2 else kept_ref
        at = k // 2 * padded
        out[at : at + padded, :] = sums_ref[pl.ds((me ^ k) * capacity, padded), :]


def unit_part(near, far, weight, hidden, experts):
    rows, width = near.shape
    slots = 2 * rows
    units = weight.shape[0]
    capacity = slots // experts
    table = jax.ShapeDtypeStruct((experts // 2 * pad8(capacity), 128), F32)
    vmem = pl.BlockSpec(memory_space=pltpu.VMEM)
    return pl.pallas_call(
        functools.partial(unit_kernel, experts, capacity),
        in_specs=[vmem] * 4,
        out_specs=[vmem] * 3,
        out_shape=[jax.ShapeDtypeStruct((slots, units), BF16), table, table],
        scratch_shapes=[
            pltpu.VMEM((slots, width), BF16),
            pltpu.VMEM((pad8(slots) + 8, 128), F32),
        ],
        compiler_params=params(),
        name="unit",
    )(near, far, weight, hidden)


def merge_kernel(plan, padded, kept_ref, got_ref, next_kept_ref, next_sent_ref):
    for out, blocks in zip((next_kept_ref, next_sent_ref), plan):
        for n, (source, block) in enumerate(blocks):
            ref = got_ref if source else kept_ref
            out[n * padded : (n + 1) * padded, :] = ref[block * padded : (block + 1) * padded, :]


def merge(kept, got, plan, padded):
    vmem = pl.BlockSpec(memory_space=pltpu.VMEM)
    return pl.pallas_call(
        functools.partial(merge_kernel, plan, padded),
        in_specs=[vmem] * 2,
        out_specs=[vmem] * 2,
        out_shape=[jax.ShapeDtypeStruct((len(blocks) * padded, 128), F32) for blocks in plan],
        compiler_params=params(),
        name="merge",
    )(kept, got)


def return_tables(kept, sent, experts, padded):
    slots, origins, bit = list(range(0, experts, 2)), [0], 1
    while True:
        got = lax.ppermute(sent, "expert", [(i, i ^ bit) for i in range(experts)])
        if len(slots) == 1:
            return [kept, got], origins + [o ^ bit for o in origins]
        width = len(origins)
        bit *= 2

        def blocks(wanted):
            return [
                (source, i * width + o)
                for i, slot in enumerate(slots)
                if bool(slot & bit) == wanted
                for source in range(2)
                for o in range(width)
            ]

        kept, sent = merge(kept, got, (blocks(False), blocks(True)), padded)
        origins = origins + [o ^ (bit // 2) for o in origins]
        slots = [slot for slot in slots if not slot & bit]


def partial_kernel(depth, left_ref, *refs):
    count = (len(refs) - 1) // 3 * 2
    rows, outs, right_ref = refs[:count], refs[count:-1], refs[-1]
    slots = rows[0].shape[0]
    for n, row in enumerate(rows):
        right_ref[n * depth : n * depth + slots, :] = row[...]
        if slots < depth:
            right_ref[n * depth + slots : (n + 1) * depth, :] = jnp.zeros(
                (depth - slots, right_ref.shape[1]), BF16
            )
    height = outs[0].shape[0]
    total = jnp.dot(left_ref[...], right_ref[...], preferred_element_type=F32)
    for n, out in enumerate(outs):
        out[...] = total[n * height : (n + 1) * height, :].astype(out.dtype)


def partial(left, rows, depth):
    count = len(rows)
    half = rows[0].shape[1]
    owners = count // 2
    height = left.shape[0] // owners
    vmem = pl.BlockSpec(memory_space=pltpu.VMEM)
    return pl.pallas_call(
        functools.partial(partial_kernel, depth),
        in_specs=[vmem] * (1 + count),
        out_specs=[vmem] * owners,
        out_shape=[jax.ShapeDtypeStruct((height, half), F32 if n == 0 else BF16) for n in range(owners)],
        scratch_shapes=[pltpu.VMEM((count * depth, half), BF16)],
        compiler_params=params(),
        name="partial",
    )(left, *rows)


def gather_masks(side):
    inner = [(d * 2) for d in range(1, side)]
    outer = [(d * side * 2) for d in range(1, side)]
    same = [(i, o) for i, o in zip(inner, outer)]
    cross = [(o ^ 1, i ^ 1) for i, o in zip(inner, outer)]
    return same, cross


def owner_masks(side):
    same = [(d * side * 2, d * 2) for d in range(1, side)]
    cross = [(a ^ 1, b ^ 1) for a, b in same]
    return [(0, 0), (1, 1)] + same + cross


def exchange(value, count, mask):
    pairs = [(i, i ^ mask[i % 2]) for i in range(count)]
    return lax.ppermute(value, "dp", pairs)


def total_kernel(terms, own_ref, *refs):
    own_terms, other_terms, out_ref = refs[:terms], refs[terms:-1], refs[-1]
    core = lax.axis_index("dp") % 2
    half = own_ref.shape[1]
    own = own_ref[...]
    for term in own_terms:
        own += term[...].astype(F32)
    other = other_terms[0][...].astype(F32)
    for term in other_terms[1:]:
        other += term[...].astype(F32)
    out_ref[:, pl.ds(pl.multiple_of(core * half, 128), half)] = own
    out_ref[:, pl.ds(pl.multiple_of((1 - core) * half, 128), half)] = other


def total(own, own_terms, other_terms):
    height, half = own.shape
    vmem = pl.BlockSpec(memory_space=pltpu.VMEM)
    return pl.pallas_call(
        functools.partial(total_kernel, len(own_terms)),
        in_specs=[vmem] * (1 + len(own_terms) + len(other_terms)),
        out_specs=vmem,
        out_shape=jax.ShapeDtypeStruct((height, 2 * half), F32),
        compiler_params=params(),
        name="total",
    )(own, *own_terms, *other_terms)


def gate_kernel(origins, padded, *refs):
    tables = refs[:-4]
    ids_ref, slots_ref, gates_ref, out_ref = refs[-4:]
    experts = len(origins)
    me = lax.axis_index("expert")
    lanes = tables[0].shape[1]
    ids = ids_ref[...]
    slots = slots_ref[...]
    gates = gates_ref[...].astype(F32)
    valid = (ids < experts) & (slots >= 0)
    place = ids ^ me
    if list(origins) != list(range(experts)):
        place = sum(jnp.where(place == o, n, 0) for n, o in enumerate(origins))
    target = jnp.where(valid, place * padded + slots, -1)
    column = jnp.concatenate([table[...] for table in tables], axis=0)
    row = lax.broadcasted_iota(jnp.int32, column.shape, 0)
    for c in range(0, ids.shape[1], lanes):
        found = [
            jnp.sum(jnp.where(row == target[k : k + 1, c : c + lanes], column, 0.0), axis=0, keepdims=True)
            for k in range(ids.shape[0])
        ]
        out_ref[:, c : c + lanes] = jnp.concatenate(found, axis=0) / gates[:, c : c + lanes]


def gate_part(tables, origins, ids, slots, gates):
    vmem = pl.BlockSpec(memory_space=pltpu.VMEM)
    padded = sum(t.shape[0] for t in tables) // len(origins)
    return pl.pallas_call(
        functools.partial(gate_kernel, tuple(origins), padded),
        in_specs=[vmem] * (len(tables) + 3),
        out_specs=vmem,
        out_shape=jax.ShapeDtypeStruct(ids.shape, F32),
        compiler_params=params(),
        name="gate",
    )(*tables, ids, slots, gates)


def on_device(out_grad, gates, expert_ids, route_slots, saved_hidden, down_weight):
    experts = lax.axis_size("expert")
    replicas = lax.axis_size("dp")
    side = math.isqrt(replicas // 2)
    assert 2 * side * side == replicas
    hidden = saved_hidden[0, 0]
    weight = down_weight[0]
    capacity = hidden.shape[0] // experts
    ids, slots, gate = expert_ids[0].T, route_slots[0].T, gates[0].T

    sent = pack(ids, slots, gate, out_grad[0], experts, pad8(capacity))
    blocks = [sent[0]]
    for k in range(1, experts):
        pairs = [(i, i ^ k) for i in range(experts)]
        blocks.append(lax.ppermute(sent[k], "expert", pairs))

    same, cross = gather_masks(side)
    routes = [(1, 1)] + same + cross
    moved_hiddens = []
    for mask in routes:
        moved_hiddens.append(exchange(hidden, replicas, mask))

    depth = -(-hidden.shape[0] // 32) * 16
    height = hidden.shape[1] // replicas
    weight, hidden = load(weight, hidden)
    left = stack([hidden] + moved_hiddens, side, depth, height)

    parts, rows = [], []
    for first in (0, experts // 2):
        part, own, other = join(blocks[first : first + experts // 2], first, capacity)
        parts.append(part)
        rows.append([own])
        for mask in routes:
            rows[-1].append(exchange(own if mask in same else other, replicas, mask))

    hidden_grad, kept, sent = unit_part(*parts, weight, hidden, experts)
    tables, origins = return_tables(kept, sent, experts, pad8(capacity))

    cut = partial(left, [r for pair in zip(*rows) for r in pair], depth)
    moved = []
    for n, mask in enumerate(owner_masks(side)[1:]):
        moved.append(exchange(cut[n + 1], replicas, mask))
    weight_grad = total(cut[0], moved[1:side], [moved[0]] + moved[side:])

    gate_grad = gate_part(tables, origins, ids, slots, gate)
    return hidden_grad[None, None], weight_grad[None], gate_grad.T[None]


def solution(mesh):
    in_specs = (
        P("dp", "expert", None),
        P("dp", "expert", None),
        P("dp", "expert", None),
        P("dp", "expert", None),
        P("dp", "expert", None, None),
        P("expert", None, None),
    )
    out_specs = (P("dp", "expert", None, None), P("expert", "dp", None), P("dp", "expert", None))
    return jax.shard_map(
        on_device, mesh=mesh, in_specs=in_specs, out_specs=out_specs, check_vma=False
    )
```

```python
import functools
import math

import jax
import jax.numpy as jnp
from jax import lax
from jax.experimental import pallas as pl
from jax.experimental.pallas import tpu as pltpu
from jax.sharding import PartitionSpec as P


F32 = jnp.float32
BF16 = jnp.bfloat16
LIMIT = 24 * 1024 * 1024
CHUNKS = 8


def params(**kw):
    return pltpu.CompilerParams(vmem_limit_bytes=LIMIT, **kw)


def in_hbm(x):
    return pltpu.with_memory_space_constraint(x, pltpu.HBM)


def pad8(n):
    return -(-n // 8) * 8


def matmul_t(a, b, contract):
    return lax.dot_general(a, b, ((contract[:1], contract[1:]), ((), ())), preferred_element_type=F32)


def pack_kernel(experts, capacity, pieces, *refs):
    arrays, out_refs = refs[:4], refs[4 : 4 + experts]
    ids_ref, slots_ref, gates_ref, grad_ref, dense_ref, small_sems, grad_sems = refs[4 + experts :]
    padded = pad8(capacity)
    chunk = dense_ref.shape[2]
    small = [
        pltpu.make_async_copy(src, dst, small_sems.at[n])
        for n, (src, dst) in enumerate(zip(arrays[:3], (ids_ref, slots_ref, gates_ref)))
    ]
    for copy in small:
        copy.start()
    width = grad_ref.shape[1] // pieces
    large = []
    for n in range(pieces):
        columns = pl.ds(n * width, width)
        large.append(
            pltpu.make_async_copy(arrays[3].at[:, columns], grad_ref.at[:, columns], grad_sems.at[n])
        )
        large[-1].start()
    for copy in small:
        copy.wait()
    me = lax.axis_index("expert")
    ids = ids_ref[...]
    slots = slots_ref[...]
    gates = gates_ref[...].astype(F32)
    valid = (ids < experts) & (slots >= 0)
    target = jnp.where(valid, (ids ^ me) * padded + slots, -1)
    row = lax.broadcasted_iota(jnp.int32, (experts * padded, ids.shape[1]), 0)
    chosen = jnp.zeros(row.shape, F32)
    for k in range(ids.shape[0]):
        chosen = jnp.where(row == target[k : k + 1, :], gates[k : k + 1, :], chosen)
    chosen = chosen.astype(BF16)
    for n in range(pieces):
        columns = slice(n * width, (n + 1) * width)
        large[n].wait()
        rows = jnp.dot(chosen, grad_ref[:, columns], preferred_element_type=F32)
        for k in range(experts):
            for c in range(CHUNKS // pieces):
                at = (n * (CHUNKS // pieces) + c) * capacity
                dense_ref[k, at : at + capacity, :] = rows[
                    k * padded : k * padded + capacity, c * chunk : (c + 1) * chunk
                ]
    for k, out in enumerate(out_refs):
        out[...] = dense_ref[k].astype(BF16)


def pack(ids, slots, gates, grad, experts, capacity):
    dense = (CHUNKS * capacity, grad.shape[1] // CHUNKS)
    pieces = 4
    arrays = (ids, slots, gates, grad)
    return pl.pallas_call(
        functools.partial(pack_kernel, experts, capacity, pieces),
        in_specs=[pl.BlockSpec(memory_space=pltpu.HBM)] * 4,
        out_specs=[pl.BlockSpec(memory_space=pltpu.VMEM)] * experts,
        out_shape=[jax.ShapeDtypeStruct(dense, BF16)] * experts,
        scratch_shapes=[pltpu.VMEM(a.shape, a.dtype) for a in arrays]
        + [pltpu.VMEM((experts, *dense), F32), pltpu.SemaphoreType.DMA((3,)), pltpu.SemaphoreType.DMA((pieces,))],
        compiler_params=params(),
        name="pack",
    )(*map(in_hbm, arrays))


def rows_of(block, first, rows, capacity):
    shape = (CHUNKS, -(-rows // 16) * 16, CHUNKS * capacity)
    chunk = lax.broadcasted_iota(jnp.int32, shape, 0)
    slot = lax.broadcasted_iota(jnp.int32, shape, 1) - first
    source = lax.broadcasted_iota(jnp.int32, shape, 2)
    place = (source == chunk * capacity + slot) & (slot >= 0) & (slot < capacity)
    place = place.astype(BF16).reshape(shape[0] * shape[1], shape[2])
    return jnp.dot(place, block[...], preferred_element_type=F32)


def join_kernel(first, capacity, *refs):
    count = len(refs) - 3
    me = lax.axis_index("expert")
    core = lax.axis_index("dp") % 2
    part_ref, own_ref, other_ref = refs[count:]
    rows, half = own_ref.shape
    total = 0.0
    for k, block in enumerate(refs[:count]):
        total += rows_of(block, ((me ^ (first + k)) % count) * capacity, rows, capacity)
    tall, chunk = total.shape[0] // CHUNKS, total.shape[1]
    for c in range(CHUNKS):
        part_ref[:, c * chunk : (c + 1) * chunk] = total[c * tall : c * tall + rows, :].astype(BF16)
    own_ref[...] = part_ref[:, pl.ds(pl.multiple_of(core * half, 128), half)]
    other_ref[...] = part_ref[:, pl.ds(pl.multiple_of((1 - core) * half, 128), half)]


def join(blocks, first, capacity):
    rows, width = len(blocks) * capacity, blocks[0].shape[1] * CHUNKS
    vmem = pl.BlockSpec(memory_space=pltpu.VMEM)
    return pl.pallas_call(
        functools.partial(join_kernel, first, capacity),
        in_specs=[vmem] * len(blocks),
        out_specs=[vmem] * 3,
        out_shape=[jax.ShapeDtypeStruct((rows, w), BF16) for w in (width, width // 2, width // 2)],
        compiler_params=params(),
        name="join",
    )(*blocks)


def load_kernel(weight_hbm, hidden_hbm, weight_ref, hidden_ref, sems):
    copies = [
        pltpu.make_async_copy(weight_hbm, weight_ref, sems.at[0]),
        pltpu.make_async_copy(hidden_hbm, hidden_ref, sems.at[1]),
    ]
    for copy in copies:
        copy.start()
    for copy in copies:
        copy.wait()


def load(weight, hidden):
    return pl.pallas_call(
        load_kernel,
        in_specs=[pl.BlockSpec(memory_space=pltpu.HBM)] * 2,
        out_specs=[pl.BlockSpec(memory_space=pltpu.VMEM)] * 2,
        out_shape=[jax.ShapeDtypeStruct(a.shape, a.dtype) for a in (weight, hidden)],
        scratch_shapes=[pltpu.SemaphoreType.DMA((2,))],
        compiler_params=params(),
        name="load",
    )(in_hbm(weight), in_hbm(hidden))


def stack_kernel(side, count, depth, *refs):
    hiddens, (left_ref, stack_ref, turned_ref) = refs[:count], refs[count:]
    slots, units = hiddens[0].shape
    rows = slots // 2
    upper = lax.axis_index("expert") // (lax.axis_size("expert") // 2)
    for n, hidden in enumerate(hiddens):
        values = hidden[...].astype(F32)
        lower, higher = values[:rows, :], values[rows:, :]
        for part in range(2):
            at = (2 * n + part) * depth
            stack_ref[at : at + rows, :] = jnp.where(upper == part, lower, higher)
            if rows < depth:
                stack_ref[at + rows : at + depth, :] = jnp.zeros((depth - rows, units), F32)
    turned_ref[...] = stack_ref[...].T
    index = lax.axis_index("dp")
    masks = owner_masks(side)
    height = left_ref.shape[0] // len(masks)
    for n, mask in enumerate(masks):
        owner = index ^ jnp.where(index % 2 == 0, mask[0], mask[1])
        start = pl.multiple_of(owner * height, 8)
        left_ref[n * height : (n + 1) * height, :] = turned_ref[pl.ds(start, height), :].astype(BF16)


def stack(hiddens, side, depth, height):
    count = len(hiddens)
    _, units = hiddens[0].shape
    vmem = pl.BlockSpec(memory_space=pltpu.VMEM)
    return pl.pallas_call(
        functools.partial(stack_kernel, side, count, depth),
        in_specs=[vmem] * count,
        out_specs=vmem,
        out_shape=jax.ShapeDtypeStruct((2 * side * height, 2 * count * depth), BF16),
        scratch_shapes=[
            pltpu.VMEM((2 * count * depth, units), F32),
            pltpu.VMEM((units, 2 * count * depth), F32),
        ],
        compiler_params=params(),
        name="stack",
    )(*hiddens)


def unit_kernel(experts, capacity, near_ref, far_ref, weight_ref, hidden_ref, *refs):
    grad_ref, kept_ref, sent_ref, full_ref, sums_ref = refs
    me = lax.axis_index("expert")
    rows = near_ref.shape[0]
    lower = me // (experts // 2) == 0
    near = near_ref[...]
    far = far_ref[...]
    full_ref[:rows, :] = jnp.where(lower, near, far)
    full_ref[rows : 2 * rows, :] = jnp.where(lower, far, near)
    unit = matmul_t(full_ref[...], weight_ref[...], (1, 1))
    grad_ref[...] = unit.astype(BF16)
    sums = jnp.sum(unit * hidden_ref[...].astype(F32), axis=1, keepdims=True)
    sums_ref[...] = jnp.zeros_like(sums_ref)
    sums_ref[: sums.shape[0], :] = jnp.broadcast_to(sums, (sums.shape[0], sums_ref.shape[1]))
    padded = pad8(capacity)
    for k in range(experts):
        out = sent_ref if k % 2 else kept_ref
        at = k // 2 * padded
        out[at : at + padded, :] = sums_ref[pl.ds((me ^ k) * capacity, padded), :]


def unit_part(near, far, weight, hidden, experts):
    rows, width = near.shape
    slots = 2 * rows
    units = weight.shape[0]
    capacity = slots // experts
    table = jax.ShapeDtypeStruct((experts // 2 * pad8(capacity), 128), F32)
    vmem = pl.BlockSpec(memory_space=pltpu.VMEM)
    return pl.pallas_call(
        functools.partial(unit_kernel, experts, capacity),
        in_specs=[vmem] * 4,
        out_specs=[vmem] * 3,
        out_shape=[jax.ShapeDtypeStruct((slots, units), BF16), table, table],
        scratch_shapes=[
            pltpu.VMEM((slots, width), BF16),
            pltpu.VMEM((pad8(slots) + 8, 128), F32),
        ],
        compiler_params=params(),
        name="unit",
    )(near, far, weight, hidden)


def merge_kernel(plan, padded, kept_ref, got_ref, next_kept_ref, next_sent_ref):
    for out, blocks in zip((next_kept_ref, next_sent_ref), plan):
        for n, (source, block) in enumerate(blocks):
            ref = got_ref if source else kept_ref
            out[n * padded : (n + 1) * padded, :] = ref[block * padded : (block + 1) * padded, :]


def merge(kept, got, plan, padded):
    vmem = pl.BlockSpec(memory_space=pltpu.VMEM)
    return pl.pallas_call(
        functools.partial(merge_kernel, plan, padded),
        in_specs=[vmem] * 2,
        out_specs=[vmem] * 2,
        out_shape=[jax.ShapeDtypeStruct((len(blocks) * padded, 128), F32) for blocks in plan],
        compiler_params=params(),
        name="merge",
    )(kept, got)


def return_tables(kept, sent, experts, padded):
    slots, origins, bit = list(range(0, experts, 2)), [0], 1
    while True:
        got = lax.ppermute(sent, "expert", [(i, i ^ bit) for i in range(experts)])
        if len(slots) == 1:
            return [kept, got], origins + [o ^ bit for o in origins]
        width = len(origins)
        bit *= 2

        def blocks(wanted):
            return [
                (source, i * width + o)
                for i, slot in enumerate(slots)
                if bool(slot & bit) == wanted
                for source in range(2)
                for o in range(width)
            ]

        kept, sent = merge(kept, got, (blocks(False), blocks(True)), padded)
        origins = origins + [o ^ (bit // 2) for o in origins]
        slots = [slot for slot in slots if not slot & bit]


def partial_kernel(depth, left_ref, *refs):
    count = (len(refs) - 1) // 3 * 2
    rows, outs, right_ref = refs[:count], refs[count:-1], refs[-1]
    slots = rows[0].shape[0]
    for n, row in enumerate(rows):
        right_ref[n * depth : n * depth + slots, :] = row[...]
        if slots < depth:
            right_ref[n * depth + slots : (n + 1) * depth, :] = jnp.zeros(
                (depth - slots, right_ref.shape[1]), BF16
            )
    height = outs[0].shape[0]
    total = jnp.dot(left_ref[...], right_ref[...], preferred_element_type=F32)
    for n, out in enumerate(outs):
        out[...] = total[n * height : (n + 1) * height, :].astype(out.dtype)


def partial(left, rows, depth):
    count = len(rows)
    half = rows[0].shape[1]
    owners = count // 2
    height = left.shape[0] // owners
    vmem = pl.BlockSpec(memory_space=pltpu.VMEM)
    return pl.pallas_call(
        functools.partial(partial_kernel, depth),
        in_specs=[vmem] * (1 + count),
        out_specs=[vmem] * owners,
        out_shape=[jax.ShapeDtypeStruct((height, half), F32 if n == 0 else BF16) for n in range(owners)],
        scratch_shapes=[pltpu.VMEM((count * depth, half), BF16)],
        compiler_params=params(),
        name="partial",
    )(left, *rows)


def gather_masks(side):
    inner = [(d * 2) for d in range(1, side)]
    outer = [(d * side * 2) for d in range(1, side)]
    same = [(i, o) for i, o in zip(inner, outer)]
    cross = [(o ^ 1, i ^ 1) for i, o in zip(inner, outer)]
    return same, cross


def owner_masks(side):
    same = [(d * side * 2, d * 2) for d in range(1, side)]
    cross = [(a ^ 1, b ^ 1) for a, b in same]
    return [(0, 0), (1, 1)] + same + cross


def exchange(value, count, mask):
    pairs = [(i, i ^ mask[i % 2]) for i in range(count)]
    return lax.ppermute(value, "dp", pairs)


def finish_kernel(terms, origins, *refs):
    own_ref, own_terms, other_terms = refs[0], refs[1 : 1 + terms], refs[1 + terms : 2 + 2 * terms]
    refs = refs[2 + 2 * terms :]
    tables, ids_ref, slots_ref, gates_ref, hidden_ref = refs[:2], *refs[2:6]
    weight_out, gate_out, hidden_out, halves_ref, gate_ref, sems = refs[6:]
    core = lax.axis_index("dp") % 2
    half = own_ref.shape[1]

    def store(src, dst, n):
        copy = pltpu.make_async_copy(src, dst, sems.at[n])
        copy.start()
        return copy

    total = own_ref[...]
    for term in own_terms:
        total += term[...].astype(F32)
    halves_ref[0] = total
    columns = pl.ds(pl.multiple_of(core * half, 128), half)
    copies = [store(halves_ref.at[0], weight_out.at[:, columns], 0)]
    total = other_terms[0][...].astype(F32)
    for term in other_terms[1:]:
        total += term[...].astype(F32)
    halves_ref[1] = total
    columns = pl.ds(pl.multiple_of((1 - core) * half, 128), half)
    copies.append(store(halves_ref.at[1], weight_out.at[:, columns], 1))
    copies.append(store(hidden_ref, hidden_out, 2))

    experts = len(origins)
    me = lax.axis_index("expert")
    lanes = tables[0].shape[1]
    padded = 2 * tables[0].shape[0] // experts
    ids = ids_ref[...]
    slots = slots_ref[...]
    gates = gates_ref[...].astype(F32)
    valid = (ids < experts) & (slots >= 0)
    place = ids ^ me
    if list(origins) != list(range(experts)):
        place = sum(jnp.where(place == o, n, 0) for n, o in enumerate(origins))
    target = jnp.where(valid, place * padded + slots, -1)
    column = jnp.concatenate([table[...] for table in tables], axis=0)
    row = lax.broadcasted_iota(jnp.int32, column.shape, 0)
    for c in range(0, ids.shape[1], lanes):
        found = [
            jnp.sum(jnp.where(row == target[k : k + 1, c : c + lanes], column, 0.0), axis=0, keepdims=True)
            for k in range(ids.shape[0])
        ]
        gate_ref[:, c : c + lanes] = jnp.concatenate(found, axis=0) / gates[:, c : c + lanes]
    copies.append(store(gate_ref, gate_out, 3))
    for copy in copies:
        copy.wait()


def finish(own, own_terms, other_terms, tables, origins, ids, slots, gates, hidden_grad):
    height, half = own.shape
    vmem = pl.BlockSpec(memory_space=pltpu.VMEM)
    hbm = pl.BlockSpec(memory_space=pltpu.HBM)
    arrays = (own, *own_terms, *other_terms, *tables, ids, slots, gates, hidden_grad)
    return pl.pallas_call(
        functools.partial(finish_kernel, len(own_terms), tuple(origins)),
        in_specs=[vmem] * len(arrays),
        out_specs=[hbm] * 3,
        out_shape=[
            jax.ShapeDtypeStruct((height, 2 * half), F32),
            jax.ShapeDtypeStruct(ids.shape, F32),
            jax.ShapeDtypeStruct(hidden_grad.shape, BF16),
        ],
        scratch_shapes=[
            pltpu.VMEM((2, height, half), F32),
            pltpu.VMEM(ids.shape, F32),
            pltpu.SemaphoreType.DMA((4,)),
        ],
        compiler_params=params(),
        name="finish",
    )(*arrays)


def on_device(out_grad, gates, expert_ids, route_slots, saved_hidden, down_weight):
    experts = lax.axis_size("expert")
    replicas = lax.axis_size("dp")
    side = math.isqrt(replicas // 2)
    assert 2 * side * side == replicas
    hidden = saved_hidden[0, 0]
    weight = down_weight[0]
    capacity = hidden.shape[0] // experts
    ids, slots, gate = expert_ids[0].T, route_slots[0].T, gates[0].T

    sent = pack(ids, slots, gate, out_grad[0], experts, capacity)
    blocks = [sent[0]]
    for k in range(1, experts):
        pairs = [(i, i ^ k) for i in range(experts)]
        blocks.append(lax.ppermute(sent[k], "expert", pairs))

    same, cross = gather_masks(side)
    routes = [(1, 1)] + same + cross
    moved_hiddens = []
    for mask in routes:
        moved_hiddens.append(exchange(hidden, replicas, mask))

    depth = -(-hidden.shape[0] // 32) * 16
    height = hidden.shape[1] // replicas
    weight, hidden = load(weight, hidden)
    left = stack([hidden] + moved_hiddens, side, depth, height)

    parts, rows = [], []
    for first in (0, experts // 2):
        part, own, other = join(blocks[first : first + experts // 2], first, capacity)
        parts.append(part)
        rows.append([own])
        for mask in routes:
            rows[-1].append(exchange(own if mask in same else other, replicas, mask))

    hidden_grad, kept, sent = unit_part(*parts, weight, hidden, experts)
    tables, origins = return_tables(kept, sent, experts, pad8(capacity))

    cut = partial(left, [r for pair in zip(*rows) for r in pair], depth)
    moved = []
    for n, mask in enumerate(owner_masks(side)[1:]):
        moved.append(exchange(cut[n + 1], replicas, mask))
    weight_grad, gate_grad, hidden_grad = finish(
        cut[0],
        moved[1:side],
        [moved[0]] + moved[side:],
        tables,
        origins,
        ids,
        slots,
        gate,
        hidden_grad,
    )
    return hidden_grad[None, None], weight_grad[None], gate_grad.T[None]


def solution(mesh):
    in_specs = (
        P("dp", "expert", None),
        P("dp", "expert", None),
        P("dp", "expert", None),
        P("dp", "expert", None),
        P("dp", "expert", None, None),
        P("expert", None, None),
    )
    out_specs = (P("dp", "expert", None, None), P("expert", "dp", None), P("dp", "expert", None))
    return jax.shard_map(
        on_device, mesh=mesh, in_specs=in_specs, out_specs=out_specs, check_vma=False
    )
```

```python
import functools
import math

import jax
import jax.numpy as jnp
from jax import lax
from jax.experimental import pallas as pl
from jax.experimental.pallas import tpu as pltpu
from jax.sharding import PartitionSpec as P


F32 = jnp.float32
BF16 = jnp.bfloat16
LIMIT = 24 * 1024 * 1024
CHUNKS = 8


def params(**kw):
    return pltpu.CompilerParams(vmem_limit_bytes=LIMIT, **kw)


def in_hbm(x):
    return pltpu.with_memory_space_constraint(x, pltpu.HBM)


def pad8(n):
    return -(-n // 8) * 8


def matmul_t(a, b, contract):
    return lax.dot_general(a, b, ((contract[:1], contract[1:]), ((), ())), preferred_element_type=F32)


def pack_kernel(experts, capacity, pieces, *refs):
    arrays, out_refs = refs[:4], refs[4 : 4 + experts]
    ids_ref, slots_ref, gates_ref, grad_ref, dense_ref, small_sems, grad_sems = refs[4 + experts :]
    padded = pad8(capacity)
    chunk = dense_ref.shape[2]
    small = [
        pltpu.make_async_copy(src, dst, small_sems.at[n])
        for n, (src, dst) in enumerate(zip(arrays[:3], (ids_ref, slots_ref, gates_ref)))
    ]
    for copy in small:
        copy.start()
    width = grad_ref.shape[1] // pieces
    large = []
    for n in range(pieces):
        columns = pl.ds(n * width, width)
        large.append(
            pltpu.make_async_copy(arrays[3].at[:, columns], grad_ref.at[:, columns], grad_sems.at[n])
        )
        large[-1].start()
    for copy in small:
        copy.wait()
    me = lax.axis_index("expert")
    ids = ids_ref[...]
    slots = slots_ref[...]
    gates = gates_ref[...].astype(F32)
    valid = (ids < experts) & (slots >= 0)
    target = jnp.where(valid, (ids ^ me) * padded + slots, -1)
    row = lax.broadcasted_iota(jnp.int32, (experts * padded, ids.shape[1]), 0)
    chosen = jnp.zeros(row.shape, F32)
    for k in range(ids.shape[0]):
        chosen = jnp.where(row == target[k : k + 1, :], gates[k : k + 1, :], chosen)
    chosen = chosen.astype(BF16)
    for n in range(pieces):
        columns = slice(n * width, (n + 1) * width)
        large[n].wait()
        rows = jnp.dot(chosen, grad_ref[:, columns], preferred_element_type=F32)
        for k in range(experts):
            for c in range(CHUNKS // pieces):
                at = (n * (CHUNKS // pieces) + c) * capacity
                dense_ref[k, at : at + capacity, :] = rows[
                    k * padded : k * padded + capacity, c * chunk : (c + 1) * chunk
                ]
    for k, out in enumerate(out_refs):
        out[...] = dense_ref[k].astype(BF16)


def pack(ids, slots, gates, grad, experts, capacity):
    dense = (CHUNKS * capacity, grad.shape[1] // CHUNKS)
    pieces = 2
    arrays = (ids, slots, gates, grad)
    return pl.pallas_call(
        functools.partial(pack_kernel, experts, capacity, pieces),
        in_specs=[pl.BlockSpec(memory_space=pltpu.HBM)] * 4,
        out_specs=[pl.BlockSpec(memory_space=pltpu.VMEM)] * experts,
        out_shape=[jax.ShapeDtypeStruct(dense, BF16)] * experts,
        scratch_shapes=[pltpu.VMEM(a.shape, a.dtype) for a in arrays]
        + [pltpu.VMEM((experts, *dense), F32), pltpu.SemaphoreType.DMA((3,)), pltpu.SemaphoreType.DMA((pieces,))],
        compiler_params=params(),
        name="pack",
    )(*map(in_hbm, arrays))


def reorder(pieces):
    me = lax.axis_index("expert")
    bit = 1
    while bit < len(pieces):
        swap = (me // bit) % 2 == 1
        pieces = [jnp.where(swap, pieces[n ^ bit], piece) for n, piece in enumerate(pieces)]
        bit *= 2
    return pieces


def cut_rows(values, starts, capacity):
    return [values[start : start + capacity, :] for start in starts]


def pad16(n):
    return -(-n // 16) * 16


def rows_of(block, first, rows, capacity):
    shape = (CHUNKS, pad16(rows), CHUNKS * capacity)
    chunk = lax.broadcasted_iota(jnp.int32, shape, 0)
    slot = lax.broadcasted_iota(jnp.int32, shape, 1) - first
    source = lax.broadcasted_iota(jnp.int32, shape, 2)
    place = (source == chunk * capacity + slot) & (slot >= 0) & (slot < capacity)
    place = place.astype(BF16).reshape(shape[0] * shape[1], shape[2])
    return jnp.dot(place, block[...], preferred_element_type=F32)


def join_kernel(count, capacity, *refs):
    core = lax.axis_index("dp") % 2
    extra = (len(refs) - count - 3) // 2
    before, (part_ref, own_ref, other_ref, *pair) = refs[count : count + extra], refs[count + extra :]
    rows, half = own_ref.shape
    total = 0.0
    for k, block in enumerate(refs[:count]):
        total += rows_of(block, k * capacity, rows, capacity)
    tall, chunk = total.shape[0] // CHUNKS, total.shape[1]
    for c in range(CHUNKS):
        part_ref[:, c * chunk : (c + 1) * chunk] = total[c * tall : c * tall + rows, :].astype(BF16)
    own_ref[...] = part_ref[:, pl.ds(pl.multiple_of(core * half, 128), half)]
    other_ref[...] = part_ref[:, pl.ds(pl.multiple_of((1 - core) * half, 128), half)]
    if before:
        pair[0][...] = jnp.zeros_like(pair[0])
        at = before[0].shape[0]
        pair[0][:at, :] = before[0][...]
        pair[0][pad16(at) : pad16(at) + rows, :] = other_ref[...]


def join(blocks, capacity, before=()):
    rows, width = len(blocks) * capacity, blocks[0].shape[1] * CHUNKS
    vmem = pl.BlockSpec(memory_space=pltpu.VMEM)
    return pl.pallas_call(
        functools.partial(join_kernel, len(blocks), capacity),
        in_specs=[vmem] * (len(blocks) + len(before)),
        out_specs=[vmem] * (3 + len(before)),
        out_shape=[jax.ShapeDtypeStruct((rows, w), BF16) for w in (width, width // 2, width // 2)]
        + [
            jax.ShapeDtypeStruct((pad16(b.shape[0]) + pad16(rows), b.shape[1]), BF16) for b in before
        ],
        compiler_params=params(),
        name="join",
    )(*blocks, *before)


def load_kernel(weight_hbm, hidden_hbm, weight_ref, hidden_ref, sems):
    copies = [
        pltpu.make_async_copy(weight_hbm, weight_ref, sems.at[0]),
        pltpu.make_async_copy(hidden_hbm, hidden_ref, sems.at[1]),
    ]
    for copy in copies:
        copy.start()
    for copy in copies:
        copy.wait()


def load(weight, hidden):
    return pl.pallas_call(
        load_kernel,
        in_specs=[pl.BlockSpec(memory_space=pltpu.HBM)] * 2,
        out_specs=[pl.BlockSpec(memory_space=pltpu.VMEM)] * 2,
        out_shape=[jax.ShapeDtypeStruct(a.shape, a.dtype) for a in (weight, hidden)],
        scratch_shapes=[pltpu.SemaphoreType.DMA((2,))],
        compiler_params=params(),
        name="load",
    )(in_hbm(weight), in_hbm(hidden))


def stack_kernel(side, count, depth, *refs):
    hiddens, (left_ref, stack_ref, turned_ref) = refs[:count], refs[count:]
    slots, _ = hiddens[0].shape
    experts = lax.axis_size("expert")
    capacity = slots // experts
    me = lax.axis_index("expert")
    row = lax.broadcasted_iota(jnp.int32, (depth, slots), 0)
    col = lax.broadcasted_iota(jnp.int32, (depth, slots), 1)
    place = jnp.zeros(row.shape, F32)
    for k in range(experts):
        start = k * capacity if k < experts - 1 else pad16(slots - capacity)
        inside = (row >= start) & (row < start + capacity)
        place = jnp.where(inside & (col == row - start + (me ^ k) * capacity), 1.0, place)
    place = place.astype(BF16)
    for n, hidden in enumerate(hiddens):
        stack_ref[n * depth : (n + 1) * depth, :] = jnp.dot(
            place, hidden[...], preferred_element_type=F32
        )
    turned_ref[...] = stack_ref[...].T
    index = lax.axis_index("dp")
    masks = owner_masks(side)
    height = left_ref.shape[0] // len(masks)
    for n, mask in enumerate(masks):
        owner = index ^ jnp.where(index % 2 == 0, mask[0], mask[1])
        start = pl.multiple_of(owner * height, 8)
        left_ref[n * height : (n + 1) * height, :] = turned_ref[pl.ds(start, height), :].astype(BF16)


def stack(hiddens, side, depth, height):
    count = len(hiddens)
    _, units = hiddens[0].shape
    vmem = pl.BlockSpec(memory_space=pltpu.VMEM)
    return pl.pallas_call(
        functools.partial(stack_kernel, side, count, depth),
        in_specs=[vmem] * count,
        out_specs=vmem,
        out_shape=jax.ShapeDtypeStruct((2 * side * height, count * depth), BF16),
        scratch_shapes=[
            pltpu.VMEM((count * depth, units), F32),
            pltpu.VMEM((units, count * depth), F32),
        ],
        compiler_params=params(),
        name="stack",
    )(*hiddens)


def unit_kernel(experts, capacity, near_ref, far_ref, weight_ref, hidden_ref, *refs):
    grad_ref, kept_ref, sent_ref, full_ref, unit_ref, sums_ref = refs
    me = lax.axis_index("expert")
    far_at = pad16(near_ref.shape[0])
    full_ref[: near_ref.shape[0], :] = near_ref[...]
    full_ref[far_at : far_at + capacity, :] = far_ref[...]
    moved = matmul_t(full_ref[...], weight_ref[...], (1, 1))
    starts = [n * capacity for n in range(experts - 1)] + [far_at]
    for n, piece in enumerate(reorder(cut_rows(moved, starts, capacity))):
        unit_ref[n * capacity : (n + 1) * capacity, :] = piece
    unit = unit_ref[...]
    grad_ref[...] = unit.astype(BF16)
    sums = jnp.sum(unit * hidden_ref[...].astype(F32), axis=1, keepdims=True)
    sums_ref[...] = jnp.zeros_like(sums_ref)
    sums_ref[: sums.shape[0], :] = jnp.broadcast_to(sums, (sums.shape[0], sums_ref.shape[1]))
    padded = pad8(capacity)
    for k in range(experts):
        out = sent_ref if k % 2 else kept_ref
        at = k // 2 * padded
        out[at : at + padded, :] = sums_ref[pl.ds((me ^ k) * capacity, padded), :]


def unit_part(near, far, weight, hidden, experts):
    width = near.shape[1]
    capacity = far.shape[0]
    slots = capacity * experts
    units = weight.shape[0]
    table = jax.ShapeDtypeStruct((experts // 2 * pad8(capacity), 128), F32)
    vmem = pl.BlockSpec(memory_space=pltpu.VMEM)
    return pl.pallas_call(
        functools.partial(unit_kernel, experts, capacity),
        in_specs=[vmem] * 4,
        out_specs=[vmem] * 3,
        out_shape=[jax.ShapeDtypeStruct((slots, units), BF16), table, table],
        scratch_shapes=[
            pltpu.VMEM((pad16(near.shape[0]) + pad16(capacity), width), BF16),
            pltpu.VMEM((slots, units), F32),
            pltpu.VMEM((pad8(slots) + 8, 128), F32),
        ],
        compiler_params=params(),
        name="unit",
    )(near, far, weight, hidden)


def merge_kernel(plan, padded, kept_ref, got_ref, next_kept_ref, next_sent_ref):
    for out, blocks in zip((next_kept_ref, next_sent_ref), plan):
        for n, (source, block) in enumerate(blocks):
            ref = got_ref if source else kept_ref
            out[n * padded : (n + 1) * padded, :] = ref[block * padded : (block + 1) * padded, :]


def merge(kept, got, plan, padded):
    vmem = pl.BlockSpec(memory_space=pltpu.VMEM)
    return pl.pallas_call(
        functools.partial(merge_kernel, plan, padded),
        in_specs=[vmem] * 2,
        out_specs=[vmem] * 2,
        out_shape=[jax.ShapeDtypeStruct((len(blocks) * padded, 128), F32) for blocks in plan],
        compiler_params=params(),
        name="merge",
    )(kept, got)


def return_tables(kept, sent, experts, padded):
    slots, origins, bit = list(range(0, experts, 2)), [0], 1
    while True:
        got = lax.ppermute(sent, "expert", [(i, i ^ bit) for i in range(experts)])
        if len(slots) == 1:
            return [kept, got], origins + [o ^ bit for o in origins]
        width = len(origins)
        bit *= 2

        def blocks(wanted):
            return [
                (source, i * width + o)
                for i, slot in enumerate(slots)
                if bool(slot & bit) == wanted
                for source in range(2)
                for o in range(width)
            ]

        kept, sent = merge(kept, got, (blocks(False), blocks(True)), padded)
        origins = origins + [o ^ (bit // 2) for o in origins]
        slots = [slot for slot in slots if not slot & bit]


def partial_kernel(depth, left_ref, pair_ref, *refs):
    count = (len(refs) - 2) // 3
    nears, fars, outs, right_ref = refs[:count], refs[count : 2 * count], refs[2 * count : -1], refs[-1]
    for n, (near, far) in enumerate(zip(nears, fars)):
        right_ref[n * depth : (n + 1) * depth, :] = jnp.zeros((depth, right_ref.shape[1]), BF16)
        at = n * depth
        right_ref[at : at + near.shape[0], :] = near[...]
        at += pad16(near.shape[0])
        right_ref[at : at + far.shape[0], :] = far[...]
    right_ref[count * depth :, :] = pair_ref[...]
    height = outs[0].shape[0]
    total = jnp.dot(left_ref[...], right_ref[...], preferred_element_type=F32)
    for n, out in enumerate(outs):
        out[...] = total[n * height : (n + 1) * height, :].astype(out.dtype)


def partial(left, nears, fars, pair):
    count = len(nears) + 1
    depth, half = pair.shape
    height = left.shape[0] // count
    vmem = pl.BlockSpec(memory_space=pltpu.VMEM)
    return pl.pallas_call(
        functools.partial(partial_kernel, depth),
        in_specs=[vmem] * (2 * count),
        out_specs=[vmem] * count,
        out_shape=[jax.ShapeDtypeStruct((height, half), F32 if n == 0 else BF16) for n in range(count)],
        scratch_shapes=[pltpu.VMEM((count * depth, half), BF16)],
        compiler_params=params(),
        name="partial",
    )(left, pair, *nears, *fars)


def gather_masks(side):
    inner = [(d * 2) for d in range(1, side)]
    outer = [(d * side * 2) for d in range(1, side)]
    same = [(i, o) for i, o in zip(inner, outer)]
    cross = [(o ^ 1, i ^ 1) for i, o in zip(inner, outer)]
    return same, cross


def owner_masks(side):
    same = [(d * side * 2, d * 2) for d in range(1, side)]
    cross = [(a ^ 1, b ^ 1) for a, b in same]
    return [(0, 0), (1, 1)] + same + cross


def exchange(value, count, mask):
    pairs = [(i, i ^ mask[i % 2]) for i in range(count)]
    return lax.ppermute(value, "dp", pairs)


def finish_kernel(terms, origins, *refs):
    own_ref, own_terms, other_terms = refs[0], refs[1 : 1 + terms], refs[1 + terms : 2 + 2 * terms]
    refs = refs[2 + 2 * terms :]
    tables, ids_ref, slots_ref, gates_ref, hidden_ref = refs[:2], *refs[2:6]
    weight_out, gate_out, hidden_out, halves_ref, gate_ref, sems = refs[6:]
    core = lax.axis_index("dp") % 2
    half = own_ref.shape[1]

    def store(src, dst, n):
        copy = pltpu.make_async_copy(src, dst, sems.at[n])
        copy.start()
        return copy

    total = own_ref[...]
    for term in own_terms:
        total += term[...].astype(F32)
    halves_ref[0] = total
    columns = pl.ds(pl.multiple_of(core * half, 128), half)
    copies = [store(halves_ref.at[0], weight_out.at[:, columns], 0)]
    total = other_terms[0][...].astype(F32)
    for term in other_terms[1:]:
        total += term[...].astype(F32)
    halves_ref[1] = total
    columns = pl.ds(pl.multiple_of((1 - core) * half, 128), half)
    copies.append(store(halves_ref.at[1], weight_out.at[:, columns], 1))
    copies.append(store(hidden_ref, hidden_out, 2))

    experts = len(origins)
    me = lax.axis_index("expert")
    lanes = tables[0].shape[1]
    padded = 2 * tables[0].shape[0] // experts
    ids = ids_ref[...]
    slots = slots_ref[...]
    gates = gates_ref[...].astype(F32)
    valid = (ids < experts) & (slots >= 0)
    place = ids ^ me
    if list(origins) != list(range(experts)):
        place = sum(jnp.where(place == o, n, 0) for n, o in enumerate(origins))
    target = jnp.where(valid, place * padded + slots, -1)
    column = jnp.concatenate([table[...] for table in tables], axis=0)
    row = lax.broadcasted_iota(jnp.int32, column.shape, 0)
    for c in range(0, ids.shape[1], lanes):
        found = [
            jnp.sum(jnp.where(row == target[k : k + 1, c : c + lanes], column, 0.0), axis=0, keepdims=True)
            for k in range(ids.shape[0])
        ]
        gate_ref[:, c : c + lanes] = jnp.concatenate(found, axis=0) / gates[:, c : c + lanes]
    copies.append(store(gate_ref, gate_out, 3))
    for copy in copies:
        copy.wait()


def finish(own, own_terms, other_terms, tables, origins, ids, slots, gates, hidden_grad):
    height, half = own.shape
    vmem = pl.BlockSpec(memory_space=pltpu.VMEM)
    hbm = pl.BlockSpec(memory_space=pltpu.HBM)
    arrays = (own, *own_terms, *other_terms, *tables, ids, slots, gates, hidden_grad)
    return pl.pallas_call(
        functools.partial(finish_kernel, len(own_terms), tuple(origins)),
        in_specs=[vmem] * len(arrays),
        out_specs=[hbm] * 3,
        out_shape=[
            jax.ShapeDtypeStruct((height, 2 * half), F32),
            jax.ShapeDtypeStruct(ids.shape, F32),
            jax.ShapeDtypeStruct(hidden_grad.shape, BF16),
        ],
        scratch_shapes=[
            pltpu.VMEM((2, height, half), F32),
            pltpu.VMEM(ids.shape, F32),
            pltpu.SemaphoreType.DMA((4,)),
        ],
        compiler_params=params(),
        name="finish",
    )(*arrays)


def on_device(out_grad, gates, expert_ids, route_slots, saved_hidden, down_weight):
    experts = lax.axis_size("expert")
    replicas = lax.axis_size("dp")
    side = math.isqrt(replicas // 2)
    assert 2 * side * side == replicas
    hidden = saved_hidden[0, 0]
    weight = down_weight[0]
    capacity = hidden.shape[0] // experts
    ids, slots, gate = expert_ids[0].T, route_slots[0].T, gates[0].T

    sent = pack(ids, slots, gate, out_grad[0], experts, capacity)
    blocks = [sent[0]]
    for k in range(1, experts):
        pairs = [(i, i ^ k) for i in range(experts)]
        blocks.append(lax.ppermute(sent[k], "expert", pairs))

    same, cross = gather_masks(side)
    routes = [(1, 1)] + same + cross
    moved_hiddens = []
    for mask in routes:
        moved_hiddens.append(exchange(hidden, replicas, mask))

    depth = pad16(hidden.shape[0] - capacity) + pad16(capacity)
    height = hidden.shape[1] // replicas
    weight, hidden = load(weight, hidden)
    left = stack([hidden] + moved_hiddens[1:] + moved_hiddens[:1], side, depth, height)

    parts, rows, before = [], [], []
    for received in (blocks[:-1], blocks[-1:]):
        part, own, other, *pair = join(received, capacity, before)
        parts.append(part)
        rows.append([own])
        before = [other]
        for n, mask in enumerate(routes[1:], 1):
            rows[-1].append(exchange(own if mask in same else other, replicas, mask))
    pair = exchange(pair[0], replicas, routes[0])

    hidden_grad, kept, sent = unit_part(*parts, weight, hidden, experts)
    tables, origins = return_tables(kept, sent, experts, pad8(capacity))

    cut = partial(left, *rows, pair)
    moved = []
    for n, mask in enumerate(owner_masks(side)[1:]):
        moved.append(exchange(cut[n + 1], replicas, mask))
    weight_grad, gate_grad, hidden_grad = finish(
        cut[0],
        moved[1:side],
        [moved[0]] + moved[side:],
        tables,
        origins,
        ids,
        slots,
        gate,
        hidden_grad,
    )
    return hidden_grad[None, None], weight_grad[None], gate_grad.T[None]


def solution(mesh):
    in_specs = (
        P("dp", "expert", None),
        P("dp", "expert", None),
        P("dp", "expert", None),
        P("dp", "expert", None),
        P("dp", "expert", None, None),
        P("expert", None, None),
    )
    out_specs = (P("dp", "expert", None, None), P("expert", "dp", None), P("dp", "expert", None))
    return jax.shard_map(
        on_device, mesh=mesh, in_specs=in_specs, out_specs=out_specs, check_vma=False
    )
```
